32 devices in a mesh: tm: 8 (over z, y), res: 4 (over x, core).
Axes of the slice: x: 2, y: 2, z: 4, core: 2. Of those that a mesh axis runs over, the one named last changes fastest.
Arguments:
- tokens: bfloat16 [1024, 64, 384], P('tm', 'res'), may hold values from -12 to 12, as said below
- cond_mask: int32 [1024], P('tm'), may hold values 0 or 1
- cond_embed: float32 [384], replicated, may hold values from -4 to 4
- attn_gain: float32 [384], replicated, may hold values from 0.1 to 1.9
- w_qkv: bfloat16 [384, 1152], replicated, may hold values from -3 to 3
- w_out: bfloat16 [384, 384], replicated, may hold values from -0.3125 to 0.3125
- mix_gain: float32 [384], replicated, may hold values from 0.1 to 1.9
- w_in: bfloat16 [384, 896], replicated, may hold values from -0.3125 to 0.3125
- decay_steps: int32 [1024, 64, 6], P('tm', 'res'), may hold values from 0 to 2048
- segment_ids: int32 [1024], replicated, may hold values from 0 to 1, never falling along the last dimension, each value on 1 to 768 neighbouring positions
- skip_gain: float32 [6], replicated, may hold values from 0.5 to 2
- w_mix_out: bfloat16 [384, 384], replicated, may hold values from -0.3125 to 0.3125
Outputs:
- denoised: bfloat16 [1024, 64, 384], P('tm', 'res')
The draws below stay inside these ranges and needn't reach their ends.
Inputs may be any that keep to these rules, and one draw needn't show every extreme that they name: `tokens`: rows of residues carry different overall scales. `segment_ids`: never falling; a frame whose number differs from the frame before starts a new trajectory.
All inputs are finite; a program needn't handle non-finite values. No bound on the sum of `cond_mask` on one device may be relied on, other than what follows from the above.
Results may differ from the reference program's by a relative error of at most 0.01.
Values may be sent and summed in bfloat16 or wider, within the bound.
No kernel may reach another device: no remote copies, remote signals or barrier semaphores. Data moves between devices by JAX's collectives and lax.ppermute only.
A program may use at most 320 MiB of HBM per device.

```python
import math
import jax
import jax.numpy as jnp
import numpy as np
from jax import lax

D = 384
HEADS = 6
HEAD_SIZE = 64
STATE = 64
SPAN_SNAPSHOTS = 1024
RESIDUES = 64


def draw_tokens(key, part):
    first_key, second_key = jax.random.split(key, 2)
    row_scales = jnp.exp(jax.random.uniform(second_key, (SPAN_SNAPSHOTS, RESIDUES, 1), jnp.float32, math.log(0.3), math.log(3.0)))
    base_draw = jnp.clip(jax.random.normal(first_key, (SPAN_SNAPSHOTS, RESIDUES, D), jnp.float32), -4.0, 4.0)
    return (base_draw * row_scales).astype(jnp.bfloat16)


def draw_w_qkv(key, part):
    first_key = jax.random.fold_in(key, 0)
    base_draw = jnp.clip(jax.random.normal(first_key, (D, 3 * D), jnp.float32), -4.0, 4.0) / math.sqrt(D)
    return base_draw.astype(jnp.bfloat16)


def draw_decay_steps(key, part):
    lookup_vector_count = jax.random.split(key, 6)
    axis_extents = (SPAN_SNAPSHOTS, RESIDUES, HEADS)
    fast_heads = jax.random.randint(lookup_vector_count[0], (1, RESIDUES, HEADS), 0, 2)
    fast_base = jax.random.randint(lookup_vector_count[1], (1, RESIDUES, HEADS), 48, 96)
    slow_base = jax.random.randint(lookup_vector_count[2], (1, RESIDUES, HEADS), 0, 2)
    base_steps = jnp.where(fast_heads == 1, fast_base, slow_base)
    jitter = jax.random.randint(lookup_vector_count[3], axis_extents, 0, 1024) % (base_steps + 1)
    stationary_phase_case = base_steps + jitter
    spike_offset = jax.random.randint(lookup_vector_count[4], (3,), 0, SPAN_SNAPSHOTS)
    spike_indicator = jnp.any(jnp.arange(SPAN_SNAPSHOTS)[:, None] == spike_offset[None, :], axis=1)
    spike_extent = jax.random.randint(lookup_vector_count[5], axis_extents, 2, 5) * 512
    return jnp.where(spike_indicator[:, None, None], spike_extent, stationary_phase_case).astype(jnp.int32)


def touch_ends(drawn, stream_key, least, top_value):
    index_at = [jax.random.randint(jax.random.fold_in(stream_key, axis), (), 0, length) for axis, length in enumerate(drawn.shape)]
    longest = drawn.shape.index(max(drawn.shape))
    neighbour = index_at[:longest] + [(index_at[longest] + 1) % drawn.shape[longest]] + index_at[longest + 1:]
    return drawn.at[tuple(index_at)].set(least).at[tuple(neighbour)].set(top_value)


def split_up(amount, total, bound, slope):
    weights = [(1 << 20) // math.isqrt(standing ** slope) + 1 for standing in range(2, amount + 1)]
    spare, holding = total - bound - (amount - 1), [1] * (amount - 1)
    while spare > 0:
        movable = [i for i in range(amount - 1) if holding[i] < bound]
        whole, budget = sum([weights[i] for i in movable]), spare
        for i in movable:
            extra = min(bound - holding[i], max(1, budget * weights[i] // whole), spare)
            holding[i] = holding[i] + extra
            spare = spare - extra
    return np.array([bound] + holding)


def uneven(stream_key, number_of, total, most, skew):
    if number_of == 2:
        one = jax.random.randint(stream_key, (), max(1, total - most), min(most, total - 1) + 1)
        return jnp.stack([one, total - one])
    sizes = jnp.asarray(split_up(number_of, total, most, skew), jnp.int32)
    couples = (number_of - 1) // 2
    giver, sink = sizes[1:1 + 2 * couples:2], sizes[2:2 + 2 * couples:2]
    room = jnp.minimum(giver - 1, most - sink)
    passed = jax.random.randint(jax.random.fold_in(stream_key, 1), (couples,), 0, 1 << 20) % (room + 1)
    sizes = sizes.at[1:1 + 2 * couples:2].set(giver - passed).at[2:2 + 2 * couples:2].set(sink + passed)
    return sizes[jax.random.permutation(jax.random.fold_in(stream_key, 2), number_of)]


def scatter_about(stream_key, dims, scale, bound, kind=jnp.bfloat16):
    values = scale * jax.random.normal(stream_key, dims, jnp.float32)
    return jnp.clip(values, min=-bound, max=bound).astype(kind)


def setup_inputs(seed: int = 0) -> dict:
    key_of = jax.random.split(jax.random.key(seed), 13)
    return {
        "tokens": draw_tokens(jax.random.fold_in(key_of[12], 71), 0),
        "cond_mask": touch_ends((jax.random.randint(key_of[1], (SPAN_SNAPSHOTS,), 0, 4) < 1).astype(jnp.int32), jax.random.fold_in(key_of[1], 1), 0, 1),
        "cond_embed": scatter_about(key_of[2], (D,), 1.0, 4.0, jnp.float32),
        "attn_gain": jnp.clip(1.0 + 0.18 * jax.random.normal(key_of[3], (D,), jnp.float32), 0.1, 1.9),
        "w_qkv": draw_w_qkv(jax.random.fold_in(key_of[12], 71), 0),
        "w_out": scatter_about(key_of[5], (D, D), D ** -0.5, 0.3125),
        "mix_gain": jnp.clip(1.0 + 0.18 * jax.random.normal(key_of[6], (D,), jnp.float32), 0.1, 1.9),
        "w_in": scatter_about(key_of[7], (D, 2 * D + 2 * STATE), D ** -0.5, 0.3125),
        "decay_steps": draw_decay_steps(jax.random.fold_in(key_of[12], 71), 0),
        "segment_ids": jnp.searchsorted(jnp.cumsum(uneven(key_of[9], 2, SPAN_SNAPSHOTS, SPAN_SNAPSHOTS - SPAN_SNAPSHOTS // 4, 2)), jnp.arange(SPAN_SNAPSHOTS), side="right").astype(jnp.int32),
        "skip_gain": jnp.clip(jax.random.uniform(key_of[10], (HEADS,), jnp.float32, 0.5, 2.0), 0.5, 2.0),
        "w_mix_out": scatter_about(key_of[11], (D, D), D ** -0.5, 0.3125),
    }


def rms_scale(hidden, gain_vec):
    return hidden * lax.rsqrt(lax.optimization_barrier(jnp.mean(hidden * hidden, axis=-1, keepdims=True)) + 1e-06) * gain_vec

def frame_attention(block_rows):
    query_rows = block_rows[:, 0].astype(jnp.float32)
    key_rows = block_rows[:, 1].astype(jnp.float32)
    value_rows = block_rows[:, 2].astype(jnp.float32)
    scores = jnp.einsum('rhd,shd->hrs', query_rows, key_rows) * (1.0 / math.sqrt(HEAD_SIZE))
    weights = jnp.exp(scores - lax.optimization_barrier(jnp.max(scores, axis=-1, keepdims=True)))
    totals = lax.optimization_barrier(jnp.sum(weights, axis=-1))
    summed = jnp.einsum('hrs,shd->hrd', weights.astype(jnp.bfloat16).astype(jnp.float32), value_rows)
    attended = summed / totals[..., None]
    return attended.transpose(1, 0, 2).reshape(RESIDUES, D).astype(jnp.bfloat16)

def advance(carried, inputs):
    decay_now, inner_now, write_now, read_now = inputs
    carried = decay_now[:, :, None, None] * carried + inner_now[..., None] * write_now[:, None, None, :]
    readout = jnp.einsum('rhpn,rn->rhp', carried, read_now, precision=lax.Precision.HIGHEST)
    return (carried, readout)

def reference(tokens, cond_mask, cond_embed, attn_gain, w_qkv, w_out, mix_gain, w_in, decay_steps, segment_ids, skip_gain, w_mix_out):
    hidden = tokens.astype(jnp.float32) + cond_mask.astype(jnp.float32)[:, None, None] * cond_embed[None, None, :]
    normed = rms_scale(hidden, attn_gain).astype(jnp.bfloat16)
    projected = jnp.dot(normed.reshape(-1, D), w_qkv, preferred_element_type=jnp.float32).astype(jnp.bfloat16)
    projected = projected.reshape(SPAN_SNAPSHOTS, RESIDUES, 3, HEADS, HEAD_SIZE)
    attended = lax.map(frame_attention, projected)
    mid = hidden + jnp.dot(attended.reshape(-1, D), w_out, preferred_element_type=jnp.float32).reshape(SPAN_SNAPSHOTS, RESIDUES, D)
    mixer_in = rms_scale(mid, mix_gain).astype(jnp.bfloat16)
    mixed = jnp.dot(mixer_in.reshape(-1, D), w_in, preferred_element_type=jnp.float32).astype(jnp.bfloat16)
    mixed = mixed.reshape(SPAN_SNAPSHOTS, RESIDUES, 2 * D + 2 * STATE)
    gate_part = mixed[..., :D].astype(jnp.float32)
    inner_x = mixed[..., D:2 * D].astype(jnp.float32).reshape(SPAN_SNAPSHOTS, RESIDUES, HEADS, HEAD_SIZE)
    write_map = mixed[..., 2 * D:2 * D + STATE].astype(jnp.float32)
    read_map = mixed[..., 2 * D + STATE:].astype(jnp.float32)
    continued = jnp.concatenate([jnp.zeros((1,), jnp.float32), (segment_ids[1:] == segment_ids[:-1]).astype(jnp.float32)])
    decays = (1.0 - decay_steps.astype(jnp.float32) / 4096.0) * continued[:, None, None]
    start_state = jnp.zeros((RESIDUES, HEADS, HEAD_SIZE, STATE), jnp.float32)
    final_state, readouts = lax.scan(advance, start_state, (decays, inner_x, write_map, read_map))
    mixer_scale = 1.0 / math.sqrt(SPAN_SNAPSHOTS * STATE)
    readouts = readouts * mixer_scale + skip_gain[None, None, :, None] * inner_x
    gated = (readouts.reshape(SPAN_SNAPSHOTS, RESIDUES, D) * jax.nn.silu(gate_part)).astype(jnp.bfloat16)
    result = mid + jnp.dot(gated.reshape(-1, D), w_mix_out, preferred_element_type=jnp.float32).reshape(SPAN_SNAPSHOTS, RESIDUES, D)
    return result.astype(jnp.bfloat16)
```

```python
import math

import jax
import jax.numpy as jnp
from jax import lax
from jax.experimental import pallas as pl
from jax.experimental.pallas import tpu as pltpu
from jax.sharding import PartitionSpec as P


BF16 = jnp.bfloat16
F32 = jnp.float32
LANES = 128
PART_FRAMES = 8
TILE_FRAMES = 16
GROUP = 4
HALVES = 2
CARRY_ROWS = 16


def rms_rows(rows, gain):
    mean = jnp.mean(rows * rows, axis=-1, keepdims=True)
    return rows * lax.rsqrt(mean + 1e-06) * gain


def nt_dot(a, b):
    return lax.dot_general(a, b, (((1,), (1,)), ((), ())), preferred_element_type=F32)


def tn_dot(a, b):
    return lax.dot_general(a, b, (((0,), (0,)), ((), ())), preferred_element_type=F32)


def nn_dot(a, b):
    return jnp.dot(a, b, preferred_element_type=F32)


def whole(shape):
    return pl.BlockSpec(shape, lambda i: (0,) * len(shape))


SMEM_SPEC = pl.BlockSpec(memory_space=pltpu.SMEM)
HBM_SPEC = pl.BlockSpec(memory_space=pl.ANY)


def attend_chunk(cond, scal, parts, embed, gain, w_qkv, first_frame, heads):
    peers = len(parts)
    frames, res, width = parts[0].shape
    head_size = width // heads
    keys = peers * res
    pairs = width // LANES
    inv_root = 1.0 / math.sqrt(head_size)

    def body(cond_ref, scal_ref, *refs):
        tok_refs = refs[:peers]
        embed_ref, gain_ref, w_ref = refs[peers : peers + 3]
        out_refs = refs[peers + 3 : 2 * peers + 3]
        norm_s, qkv_s = refs[2 * peers + 3 :]
        me = scal_ref[0]
        embed_row = embed_ref[...]
        gain_row = gain_ref[...]
        for f in range(frames):
            flag = cond_ref[first_frame + me * frames + f].astype(F32)
            added = flag * embed_row
            for k in range(peers):
                rows = tok_refs[k][f].astype(F32) + added
                norm_s[k, f] = rms_rows(rows, gain_row).astype(BF16)
        flat = norm_s[...].reshape(peers * frames * res, width)
        for n in range(3):
            cols = slice(n * width, (n + 1) * width)
            got = nn_dot(flat, w_ref[:, cols]).astype(BF16)
            if n == 0:
                got = got * jnp.asarray(inv_root, BF16)
            qkv_s[:, :, :, cols] = got.reshape(peers, frames, res, width)
        lane = lax.broadcasted_iota(jnp.int32, (1, LANES), 1)
        first = (lane < head_size).astype(BF16)
        second = (lane >= head_size).astype(BF16)
        pick = lax.broadcasted_iota(jnp.int32, (keys, LANES), 1) < head_size
        for f in range(frames):
            for p in range(pairs):

                def part(n):
                    lo = n * width + p * LANES
                    return qkv_s[:, f, :, lo : lo + LANES].reshape(keys, LANES)

                q, k_rows, v_rows = part(0), part(1), part(2)
                stacked = jnp.concatenate([q * first, q * second], axis=0)
                scores = nt_dot(k_rows, stacked)
                top = jnp.max(scores, axis=0, keepdims=True)
                weights = jnp.exp(scores - top)
                totals = jnp.sum(weights, axis=0, keepdims=True)
                weights = (weights * (1.0 / totals)).astype(BF16)
                both = tn_dot(weights, v_rows)
                att = jnp.where(pick, both[:keys], both[keys:]).astype(BF16)
                for k in range(peers):
                    out_refs[k][f, :, p * LANES : (p + 1) * LANES] = att[k * res : (k + 1) * res]

    block = whole((frames, res, width))
    return pl.pallas_call(
        body,
        grid=(1,),
        in_specs=[SMEM_SPEC, SMEM_SPEC]
        + [block] * peers
        + [whole((1, width)), whole((1, width)), whole(w_qkv.shape)],
        out_specs=[block] * peers,
        out_shape=[jax.ShapeDtypeStruct((frames, res, width), BF16)] * peers,
        scratch_shapes=[
            pltpu.VMEM((peers, frames, res, width), BF16),
            pltpu.VMEM((peers, frames, res, 3 * width), BF16),
        ],
        name="attend",
    )(cond, scal, *parts, embed, gain, w_qkv)


def mix_chunk(c, chunks, cond, scal, tokens, attended, steps, consts, carry, buffers, mixer_scale):
    frames_all, res, width = tokens.shape
    peers = len(attended)
    part_frames = attended[0].shape[0]
    frames = part_frames * peers
    tiles = frames // TILE_FRAMES
    rows = TILE_FRAMES * res
    state = consts["row_mask"].shape[1] // res
    spread = res * state
    last = c == chunks - 1
    per_pay = res // (GROUP * HALVES)
    pay_rows = per_pay * state
    names = ["embed", "mix_gain", "w_out", "w_in", "expand", "skip", "row_mask", "col_mask"]
    const_args = [consts[n] for n in names]
    n_in = 3 + peers + 1 + len(const_args)
    carry_args = [] if carry is None else list(carry)
    buffer_args = [] if buffers is None else list(buffers)

    def body(*refs):
        cond_ref, scal_ref, tok_ref = refs[:3]
        att_refs = refs[3 : 3 + peers]
        steps_ref = refs[3 + peers]
        embed_ref, gain_ref, wo_ref, wi_ref, ex_ref, skip_ref, rm_ref, cm_ref = refs[4 + peers : n_in]
        pos = n_in
        carry_refs = refs[pos : pos + len(carry_args)]
        pos += len(carry_args) + len(buffer_args)
        mid_ref, z_ref, ag_ref, rr_ref = refs[pos : pos + 4]
        pos += 4
        pay_refs = refs[pos : pos + GROUP * HALVES] if last else ()
        pos += len(pay_refs)
        if last:
            att_s, s_ref, p_ref, p_wide = refs[pos:]
        else:
            s_ref, p_ref, att_s = refs[pos:]
        me, place, reset = scal_ref[0], scal_ref[1], scal_ref[2]
        for k in range(peers):
            att_s[me ^ k] = att_refs[k][...]
        if carry is None:
            s_ref[...] = jnp.zeros_like(s_ref)
            p_ref[...] = jnp.ones_like(p_ref)
        else:
            s_ref[...] = carry_refs[0][...]
            p_ref[...] = carry_refs[1][...]
        embed_row = embed_ref[...]
        row_i = lax.broadcasted_iota(jnp.int32, (rows, rows), 0)
        col_i = lax.broadcasted_iota(jnp.int32, (rows, rows), 1)
        causal = ((row_i % res) == (col_i % res)) & (row_i >= col_i)
        per_tile = TILE_FRAMES // part_frames
        for i in range(tiles):
            g0 = c * frames + i * TILE_FRAMES
            g_end = g0 + TILE_FRAMES - 1
            sl = slice(i * rows, (i + 1) * rows)
            hidden = jnp.concatenate(
                [
                    tok_ref[i * TILE_FRAMES + f].astype(F32)
                    + cond_ref[g0 + f].astype(F32) * embed_row
                    for f in range(TILE_FRAMES)
                ],
                axis=0,
            )
            att = att_s[i * per_tile : (i + 1) * per_tile].reshape(rows, width)
            mid = hidden + nn_dot(att, wo_ref[...])
            mid_ref[sl] = mid
            mixer_in = rms_rows(mid, gain_ref[...]).astype(BF16)
            gate = nn_dot(mixer_in, wi_ref[:, :width]).astype(BF16).astype(F32)
            inner = nn_dot(mixer_in, wi_ref[:, width : 2 * width]).astype(BF16).astype(F32)
            maps = nn_dot(mixer_in, wi_ref[:, 2 * width :]).astype(BF16)
            ww, rr = maps[:, : 2 * state], maps[:, 2 * state :]
            rr_ref[sl] = rr
            decay = 1.0 - nn_dot(steps_ref[sl], ex_ref[...]) * (1.0 / 4096.0)
            d = [decay[f * res : (f + 1) * res] for f in range(TILE_FRAMES)]
            before = [d[0]]
            for f in range(1, TILE_FRAMES):
                before.append(before[-1] * d[f])
            after = [jnp.ones_like(d[0])]
            for f in range(TILE_FRAMES - 1, 0, -1):
                after.append(after[-1] * d[f])
            after = after[::-1]
            back = 1.0 / before[-1]
            keep_start = [
                jnp.where((reset >= g0) & (reset <= g0 + f), 0.0, 1.0).astype(F32)
                for f in range(TILE_FRAMES)
            ]
            keep_end = [
                jnp.where((reset > g0 + f) & (reset <= g_end), 0.0, 1.0).astype(F32)
                for f in range(TILE_FRAMES)
            ]
            from_base = jnp.concatenate([b * s for b, s in zip(before, keep_start)], axis=0)
            relative = jnp.concatenate([b * back for b in before], axis=0)
            inner_end = inner * jnp.concatenate(after, axis=0)
            inner_kept = jnp.concatenate(
                [
                    inner_end[f * res : (f + 1) * res] * keep_end[f]
                    for f in range(TILE_FRAMES)
                ],
                axis=0,
            ).astype(BF16)
            inner_end = inner_end.astype(BF16)
            transit = before[-1] * keep_start[-1]
            edge = (reset - g0) * res
            joined = causal & ((row_i >= edge) == (col_i >= edge))
            gram = jnp.where(joined, nt_dot(rr, ww) * 0.5, 0.0).astype(BF16)
            near = nn_dot(gram, inner_end) * relative
            read = jnp.concatenate(
                [rr * rm_ref[:, j * LANES : (j + 1) * LANES] for j in range(spread // LANES)], axis=1
            )
            far = nn_dot(read, s_ref[...].astype(BF16)) * from_base
            silu = gate / (1.0 + jnp.exp(-gate))
            z_ref[sl] = ((near + far) * mixer_scale + skip_ref[...] * inner) * silu
            start = p_ref[...]
            reach = jnp.concatenate(
                [start * from_base[f * res : (f + 1) * res] for f in range(TILE_FRAMES)], axis=0
            )
            ag_ref[sl] = (reach * silu * mixer_scale).astype(BF16)
            p_ref[...] = start * transit
            write_t = ww.astype(F32).T.astype(BF16)[:state]
            write = jnp.concatenate(
                [write_t * cm_ref[r * state : (r + 1) * state] for r in range(res)], axis=0
            )
            added = nn_dot(write, inner_kept)
            for r in range(res):
                rs = slice(r * state, (r + 1) * state)
                s_ref[rs] = s_ref[rs] * transit[r : r + 1] + added[rs]
        if not last:
            return
        p_all = p_ref[...]
        for r in range(res):
            p_wide[r] = jnp.broadcast_to(p_all[r : r + 1], (8, width))
        sub = lax.broadcasted_iota(jnp.int32, (CARRY_ROWS, width), 0) % 8
        for e in range(HALVES):
            for k in range(GROUP):
                r0 = ((place ^ k) * HALVES + e) * per_pay
                out = pay_refs[e * GROUP + k]
                start = pl.multiple_of(r0 * state, pay_rows)
                out[:pay_rows] = s_ref[pl.ds(start, pay_rows), :].astype(BF16)
                value = jnp.concatenate([p_wide[r0 + n] for n in range(per_pay)], axis=0)
                upper = value.astype(BF16).astype(F32)
                out[pay_rows:] = jnp.where(sub < 4, upper, value - upper).astype(BF16)

    chunk_tok = pl.BlockSpec((frames, res, width), lambda i: (c, 0, 0))
    chunk_rows = frames * res
    all_rows = frames_all * res

    def row_block(cols):
        return pl.BlockSpec((chunk_rows, cols), lambda i: (c, 0))

    state_specs = [whole((spread, width)), whole((res, width))]
    state_shapes = [
        jax.ShapeDtypeStruct((spread, width), F32),
        jax.ShapeDtypeStruct((res, width), F32),
    ]
    in_specs = (
        [SMEM_SPEC, SMEM_SPEC, chunk_tok]
        + [whole(attended[0].shape)] * peers
        + [row_block(LANES)]
        + [whole(a.shape) for a in const_args]
        + state_specs[: len(carry_args)]
        + [HBM_SPEC] * len(buffer_args)
    )
    out_specs = [row_block(width), row_block(width), row_block(width), row_block(LANES)]
    out_shape = [
        jax.ShapeDtypeStruct((all_rows, width), F32),
        jax.ShapeDtypeStruct((all_rows, width), F32),
        jax.ShapeDtypeStruct((all_rows, width), BF16),
        jax.ShapeDtypeStruct((all_rows, LANES), BF16),
    ]
    scratch = [pltpu.VMEM((peers, part_frames, res, width), BF16)]
    if last:
        pay = (pay_rows + CARRY_ROWS, width)
        out_specs += [whole(pay)] * (GROUP * HALVES)
        out_shape += [jax.ShapeDtypeStruct(pay, BF16)] * (GROUP * HALVES)
        scratch += [
            pltpu.VMEM((spread, width), F32),
            pltpu.VMEM((res, width), F32),
            pltpu.VMEM((res, 8, width), F32),
        ]
    else:
        out_specs += state_specs
        out_shape += state_shapes
    first_buffer = n_in + len(carry_args)
    outs = pl.pallas_call(
        body,
        grid=(1,),
        in_specs=in_specs,
        out_specs=out_specs,
        out_shape=out_shape,
        scratch_shapes=scratch,
        input_output_aliases={first_buffer + n: n for n in range(len(buffer_args))},
        name="mix",
    )(cond, scal, tokens, *attended, steps, *const_args, *carry_args, *buffer_args)
    return outs[:4], outs[4:]


def decay_rows(tail, n):
    tail = tail.astype(F32)
    return [tail[8 * i : 8 * i + 1] + tail[8 * i + 4 : 8 * i + 5] for i in range(n)]


def group_total(scal, got, state):
    pay, width = got[0].shape
    body_rows = pay - CARRY_ROWS
    n = body_rows // state

    def body(scal_ref, *refs):
        got_refs, out_ref, sorted_s = refs[:GROUP], refs[GROUP], refs[GROUP + 1]
        place = scal_ref[1]
        for k in range(GROUP):
            sorted_s[place ^ k] = got_refs[k][...]
        tails = [decay_rows(sorted_s[j, body_rows:], n) for j in range(GROUP)]
        lines = []
        for i in range(n):
            rs = slice(i * state, (i + 1) * state)
            total = sorted_s[0, rs].astype(F32)
            product = tails[0][i]
            for j in range(1, GROUP):
                total = total * tails[j][i] + sorted_s[j, rs].astype(F32)
                product = product * tails[j][i]
            out_ref[rs] = total.astype(BF16)
            lines.append(jnp.broadcast_to(product, (8, width)))
        value = jnp.concatenate(lines, axis=0)
        sub = lax.broadcasted_iota(jnp.int32, (CARRY_ROWS, width), 0) % 8
        upper = value.astype(BF16).astype(F32)
        out_ref[body_rows:] = jnp.where(sub < 4, upper, value - upper).astype(BF16)

    return pl.pallas_call(
        body,
        grid=(1,),
        in_specs=[SMEM_SPEC] + [whole((pay, width))] * GROUP,
        out_specs=whole((pay, width)),
        out_shape=jax.ShapeDtypeStruct((pay, width), BF16),
        scratch_shapes=[pltpu.VMEM((GROUP, pay, width), BF16)],
        name="group_total",
    )(scal, *got)


def group_prefixes(scal, got, entering, state):
    pay, width = got[0].shape
    body_rows = pay - CARRY_ROWS
    n = body_rows // state

    def body(scal_ref, *refs):
        got_refs, in_ref = refs[:GROUP], refs[GROUP]
        out_refs = refs[GROUP + 1 : 2 * GROUP + 1]
        sorted_s, prefix_s = refs[2 * GROUP + 1 :]
        place = scal_ref[1]
        for k in range(GROUP):
            sorted_s[place ^ k] = got_refs[k][...]
        tails = [decay_rows(sorted_s[j, body_rows:], n) for j in range(GROUP)]
        for i in range(n):
            rs = slice(i * state, (i + 1) * state)
            total = in_ref[rs].astype(F32)
            prefix_s[0, rs] = total.astype(BF16)
            for j in range(GROUP - 1):
                total = total * tails[j][i] + sorted_s[j, rs].astype(F32)
                prefix_s[j + 1, rs] = total.astype(BF16)
        for k in range(GROUP):
            out_refs[k][...] = prefix_s[place ^ k]

    spec = whole((pay, width))
    out = whole((body_rows, width))
    return pl.pallas_call(
        body,
        grid=(1,),
        in_specs=[SMEM_SPEC] + [spec] * (GROUP + 1),
        out_specs=[out] * GROUP,
        out_shape=[jax.ShapeDtypeStruct((body_rows, width), BF16)] * GROUP,
        scratch_shapes=[
            pltpu.VMEM((GROUP, pay, width), BF16),
            pltpu.VMEM((GROUP, body_rows, width), BF16),
        ],
        name="group_prefixes",
    )(scal, *got, entering)


def join_payloads(earlier, later, state):
    body_rows = later.shape[0] - CARRY_ROWS
    n = body_rows // state
    width = later.shape[1]
    early = decay_rows(earlier[body_rows:], n)
    late = decay_rows(later[body_rows:], n)
    parts, lines = [], []
    for i in range(n):
        rs = slice(i * state, (i + 1) * state)
        parts.append(earlier[rs].astype(F32) * late[i] + later[rs].astype(F32))
        value = early[i] * late[i]
        upper = value.astype(BF16).astype(F32)
        lines += [jnp.broadcast_to(upper, (4, width)), jnp.broadcast_to(value - upper, (4, width))]
    return jnp.concatenate(parts + lines, axis=0).astype(BF16)


def states_entering(scal, payloads, state, tm_size):
    groups = tm_size // GROUP

    def swap(value, k):
        return lax.ppermute(value, "tm", [(i, i ^ k) for i in range(tm_size)])

    def onward(value, hops):
        moved = hops * GROUP
        return lax.ppermute(value, "tm", [(i, i + moved) for i in range(tm_size - moved)])

    gathered = []
    for e in range(HALVES):
        mine = payloads[e * GROUP : (e + 1) * GROUP]
        gathered.append([mine[0]] + [swap(mine[k], k) for k in range(1, GROUP)])
    result = []
    for got in gathered:
        total = group_total(scal, got, state)
        entering = onward(total, 1) if groups > 1 else jnp.zeros_like(total)
        hops = 1
        while hops < groups - 1:
            entering = join_payloads(onward(entering, hops), entering, state)
            hops *= 2
        mine = group_prefixes(scal, got, entering, state)
        result.append([mine[0]] + [swap(mine[k], k) for k in range(1, GROUP)])
    return [part for half in result for part in half]


def finish(scal, entered, mid, z, ag, rr, w_mix, row_mask, frames, res):
    width = mid.shape[1]
    rows = TILE_FRAMES * res
    spread = row_mask.shape[1]
    piece = entered[0].shape[0]

    def body(scal_ref, *refs):
        n = GROUP * HALVES
        in_refs = refs[:n]
        mid_ref, z_ref, ag_ref, rr_ref, w_ref, rm_ref, out_ref, state_s = refs[n:]

        @pl.when(pl.program_id(0) == 0)
        def _():
            place = scal_ref[1]
            for e in range(HALVES):
                for k in range(GROUP):
                    state_s[(place ^ k) * HALVES + e] = in_refs[e * GROUP + k][...]

        tile = rr_ref[...]
        read = jnp.concatenate(
            [tile * rm_ref[:, j * LANES : (j + 1) * LANES] for j in range(spread // LANES)], axis=1
        )
        far = nn_dot(read, state_s[...].reshape(spread, width))
        gated = (z_ref[...] + ag_ref[...].astype(F32) * far).astype(BF16)
        out = mid_ref[...] + nn_dot(gated, w_ref[...])
        out_ref[...] = out.astype(BF16).reshape(TILE_FRAMES, res, width)

    def tile_spec(cols):
        return pl.BlockSpec((rows, cols), lambda i: (i, 0))

    return pl.pallas_call(
        body,
        grid=(frames // TILE_FRAMES,),
        in_specs=[SMEM_SPEC]
        + [whole((piece, width))] * (GROUP * HALVES)
        + [tile_spec(width), tile_spec(width), tile_spec(width), tile_spec(LANES)]
        + [whole(w_mix.shape), whole(row_mask.shape)],
        out_specs=pl.BlockSpec((TILE_FRAMES, res, width), lambda i: (i, 0, 0)),
        out_shape=jax.ShapeDtypeStruct((frames, res, width), BF16),
        scratch_shapes=[pltpu.VMEM((GROUP * HALVES, piece, width), BF16)],
        name="finish",
    )(scal, *entered, mid, z, ag, rr, w_mix, row_mask)


def local(
    tokens,
    cond_mask,
    cond_embed,
    attn_gain,
    w_qkv,
    w_out,
    mix_gain,
    w_in,
    decay_steps,
    segment_ids,
    skip_gain,
    w_mix_out,
):
    frames, res, width = tokens.shape
    heads = skip_gain.shape[0]
    head_size = width // heads
    state = (w_in.shape[1] - 2 * width) // 2
    spread = res * state
    tm_size = lax.axis_size("tm")
    peers = lax.axis_size("res")
    part = PART_FRAMES
    chunks = frames // (part * peers)
    rows = TILE_FRAMES * res
    me = lax.axis_index("res")
    block = lax.axis_index("tm")
    reset = jnp.sum((segment_ids == segment_ids[0]).astype(jnp.int32)) - block * frames
    scal = jnp.stack([me, block % GROUP, reset]).astype(jnp.int32)

    pieces = tokens.reshape(chunks, peers, part, res, width)
    order = list(range(peers - 1, 0, -1))

    def swap(value, k):
        return lax.ppermute(value, "res", [(i, i ^ k) for i in range(peers)])

    gathered = []
    for c in range(chunks):
        mine = [lax.dynamic_index_in_dim(pieces[c], me ^ k, keepdims=False) for k in range(peers)]
        got = {k: swap(mine[k], k) for k in order}
        got[0] = mine[0]
        gathered.append([got[k] for k in range(peers)])

    embed = cond_embed.reshape(1, width)
    lane_head = jnp.arange(width) // head_size
    pick = (jnp.arange(LANES)[:, None] % heads == lane_head[None, :]) & (
        jnp.arange(LANES)[:, None] < 2 * heads
    )
    scale = jnp.where(jnp.arange(LANES)[:, None] < heads, 64.0, 1.0)
    expand = jnp.where(pick, scale, 0.0).astype(BF16)
    halves = jnp.concatenate([decay_steps // 64, decay_steps % 64], axis=-1)
    steps = jnp.pad(halves.astype(BF16), ((0, 0), (0, 0), (0, LANES - 2 * heads)))
    steps = steps.reshape(frames * res, LANES)
    write_cols = w_in[:, 2 * width : 2 * width + state]
    read_cols = w_in[:, 2 * width + state :]
    w_in_wide = jnp.concatenate(
        [w_in[:, : 2 * width], write_cols, write_cols, read_cols, read_cols], axis=1
    )
    row_mask = (jnp.arange(rows)[:, None] % res == jnp.arange(spread)[None, :] // state).astype(BF16)
    col_mask = (jnp.arange(spread)[:, None] // state == jnp.arange(rows)[None, :] % res).astype(BF16)
    consts = {
        "embed": embed,
        "mix_gain": mix_gain.reshape(1, width),
        "w_out": w_out,
        "w_in": w_in_wide,
        "expand": expand,
        "skip": jnp.repeat(skip_gain, head_size).reshape(1, width),
        "row_mask": row_mask,
        "col_mask": col_mask,
    }
    mixer_scale = 1.0 / math.sqrt(frames * tm_size * state)

    attended = []
    for c in range(chunks):
        outs = attend_chunk(
            cond_mask,
            scal,
            gathered[c],
            embed,
            attn_gain.reshape(1, width),
            w_qkv,
            c * part * peers,
            heads,
        )
        back = {k: swap(outs[k], k) for k in order}
        back[0] = outs[0]
        attended.append([back[k] for k in range(peers)])

    carry, buffers = None, None
    for c in range(chunks):
        buffers, carry = mix_chunk(
            c,
            chunks,
            cond_mask,
            scal,
            tokens,
            attended[c],
            steps,
            consts,
            carry,
            buffers,
            mixer_scale,
        )
    entered = states_entering(scal, carry, state, tm_size)
    mid, z, ag, rr = buffers
    return finish(scal, entered, mid, z, ag, rr, w_mix_out, row_mask, frames, res)


def solution(mesh):
    in_specs = (
        P("tm", "res", None),
        P("tm"),
        P(),
        P(),
        P(),
        P(),
        P(),
        P(),
        P("tm", "res", None),
        P(),
        P(),
        P(),
    )
    out_specs = P("tm", "res", None)
    return jax.shard_map(local, mesh=mesh, in_specs=in_specs, out_specs=out_specs, check_vma=False)
```

```python
import math

import jax
import jax.numpy as jnp
from jax import lax
from jax.experimental import pallas as pl
from jax.experimental.pallas import tpu as pltpu
from jax.sharding import PartitionSpec as P


BF16 = jnp.bfloat16
F32 = jnp.float32
LANES = 128
PART_FRAMES = 16
STAGE_FRAMES = 2
TILE_FRAMES = 32
OCTET = 8
GROUP = 4
HALVES = 2
CARRY_ROWS = 16


def rms_rows(rows, gain):
    mean = jnp.mean(rows * rows, axis=-1, keepdims=True)
    return rows * lax.rsqrt(mean + 1e-06) * gain


def nt_dot(a, b):
    return lax.dot_general(a, b, (((1,), (1,)), ((), ())), preferred_element_type=F32)


def tn_dot(a, b):
    return lax.dot_general(a, b, (((0,), (0,)), ((), ())), preferred_element_type=F32)


def nn_dot(a, b):
    return jnp.dot(a, b, preferred_element_type=F32)


def joined_row(ref):
    return jnp.concatenate([ref[i : i + 1] for i in range(ref.shape[0])], axis=1)


def my_place():
    return lax.axis_index("tm") % GROUP


def whole(shape):
    return pl.BlockSpec(shape, lambda i: (0,) * len(shape))


def grant(mib):
    return pltpu.CompilerParams(vmem_limit_bytes=mib << 20)


SMEM_SPEC = pl.BlockSpec(memory_space=pltpu.SMEM)
HBM_SPEC = pl.BlockSpec(memory_space=pl.ANY)


def prepare(tokens, segment_ids, after, chunks, peers):
    frames, res, width = tokens.shape
    part = frames // (chunks * peers)
    count = chunks * peers

    def body(*refs):
        tok_ref, ids_ref = refs[:2]
        reset_ref, out_refs = refs[-1 - count], refs[-count:]
        me = lax.axis_index("res")
        for c in range(chunks):
            for k in range(peers):
                start = c * part * peers + (me ^ k) * part
                out_refs[c * peers + k][...] = tok_ref[pl.ds(start, part)]
        ids = ids_ref[...]
        first = (ids == jnp.min(ids)).astype(F32)
        lead = jnp.sum(first).astype(jnp.int32)
        reset_ref[0] = lead - lax.axis_index("tm") * frames

    piece = (part, res, width)
    outs = pl.pallas_call(
        body,
        grid=(1,),
        in_specs=[whole(tokens.shape), whole(segment_ids.shape)] + [HBM_SPEC] * len(after),
        out_specs=[SMEM_SPEC] + [whole(piece)] * count,
        out_shape=[jax.ShapeDtypeStruct((1,), jnp.int32)]
        + [jax.ShapeDtypeStruct(piece, tokens.dtype)] * count,
        compiler_params=grant(10),
        name="prepare",
    )(tokens, segment_ids, *after)
    return outs[0], outs[1:]


def attend_chunk(cond, parts, embed, gain, w_qkv, first_frame, heads):
    peers = len(parts)
    frames, res, width = parts[0].shape
    head_size = width // heads
    keys = peers * res
    pairs = width // LANES
    inv_root = 1.0 / math.sqrt(head_size)

    def body(cond_ref, *refs):
        tok_refs = refs[:peers]
        embed_ref, gain_ref, w_ref = refs[peers : peers + 3]
        out_refs = refs[peers + 3 : 2 * peers + 3]
        norm_s, qkv_s = refs[2 * peers + 3 :]
        me = lax.axis_index("res")
        embed_row = joined_row(embed_ref)
        gain_row = joined_row(gain_ref)
        for f in range(frames):
            flag = cond_ref[first_frame + me * frames + f].astype(F32)
            added = flag * embed_row
            for k in range(peers):
                rows = tok_refs[k][f].astype(F32) + added
                norm_s[k, f] = rms_rows(rows, gain_row).astype(BF16)
        flat = norm_s[...].reshape(peers * frames * res, width)
        shape = (peers, frames, res)
        got = nn_dot(flat, w_ref[:, : 2 * width]).astype(BF16)
        scaled = got[:, :width] * jnp.asarray(inv_root, BF16)
        qkv_s[:, :, :, :width] = scaled.reshape(*shape, width)
        qkv_s[:, :, :, width : 2 * width] = got[:, width:].reshape(*shape, width)
        got = nn_dot(flat, w_ref[:, 2 * width :]).astype(BF16)
        qkv_s[:, :, :, 2 * width :] = got.reshape(*shape, width)
        lane = lax.broadcasted_iota(jnp.int32, (1, LANES), 1)
        first = (lane < head_size).astype(BF16)
        second = (lane >= head_size).astype(BF16)
        pick = lax.broadcasted_iota(jnp.int32, (keys, LANES), 1) < head_size

        def stage(f0):
            units = [(f0 + f, p) for f in range(STAGE_FRAMES) for p in range(pairs)]

            def part(n, f, p):
                lo = n * width + p * LANES
                return qkv_s[:, pl.ds(f, 1), :, lo : lo + LANES].reshape(keys, LANES)

            scores = []
            for f, p in units:
                q = part(0, f, p)
                stacked = jnp.concatenate([q * first, q * second], axis=0)
                scores.append(nt_dot(part(1, f, p), stacked))
            tops = [jnp.max(x, axis=0, keepdims=True) for x in scores]
            weights = [jnp.exp(x - t) for x, t in zip(scores, tops)]
            totals = [jnp.sum(w, axis=0, keepdims=True) for w in weights]
            weights = [(w * (1.0 / t)).astype(BF16) for w, t in zip(weights, totals)]
            both = [tn_dot(w, part(2, f, p)) for w, (f, p) in zip(weights, units)]
            for got, (f, p) in zip(both, units):
                att = jnp.where(pick, got[:keys], got[keys:]).astype(BF16)
                for k in range(peers):
                    out_refs[k][pl.ds(f, 1), :, p * LANES : (p + 1) * LANES] = att[
                        k * res : (k + 1) * res
                    ].reshape(1, res, LANES)

        def step(i, _):
            stage(i * STAGE_FRAMES)
            return 0

        lax.fori_loop(0, frames // STAGE_FRAMES, step, 0, unroll=2)

    block = whole((frames, res, width))
    return pl.pallas_call(
        body,
        grid=(1,),
        in_specs=[SMEM_SPEC]
        + [block] * peers
        + [whole(a.shape) for a in (embed, gain, w_qkv)],
        out_specs=[block] * peers,
        out_shape=[jax.ShapeDtypeStruct((frames, res, width), BF16)] * peers,
        scratch_shapes=[
            pltpu.VMEM((peers, frames, res, width), BF16),
            pltpu.VMEM((peers, frames, res, 3 * width), BF16),
        ],
        compiler_params=grant(14),
        name="attend",
    )(cond, *parts, embed, gain, w_qkv)


def octets(rows, frames, res):
    n = rows.shape[-1]
    cube = rows.reshape(frames, res, n)
    return [
        cube[:, o * OCTET : (o + 1) * OCTET].reshape(frames * OCTET, n) for o in range(res // OCTET)
    ]


def wide_decays(steps, heads, width):
    values = 1.0 - steps.astype(F32) * (1.0 / 4096.0)
    rows = values.shape[0]
    head_size = width // heads
    per = LANES // head_size
    lane_head = lax.broadcasted_iota(jnp.int32, (rows, LANES), 1) // head_size
    parts = []
    for p in range(width // LANES):
        part = jnp.broadcast_to(values[:, p * per : p * per + 1], (rows, LANES))
        for h in range(1, per):
            col = values[:, p * per + h : p * per + h + 1]
            part = jnp.where(lane_head == h, jnp.broadcast_to(col, (rows, LANES)), part)
        parts.append(part)
    return jnp.concatenate(parts, axis=1)


def frame_rows(value, f):
    return value[f * OCTET : (f + 1) * OCTET]


def twice_each(maps, state):
    low = lax.broadcasted_iota(jnp.int32, maps.shape, 1) < state
    turned = pltpu.roll(maps, state, 1)
    return jnp.where(low, maps, turned), jnp.where(low, turned, maps)


def spread_read(rr, state):
    rows = rr.shape[0]
    mine = lax.broadcasted_iota(jnp.int32, (rows, LANES), 0) % OCTET
    lane = lax.broadcasted_iota(jnp.int32, (rows, LANES), 1) // state
    per = LANES // state
    return jnp.concatenate(
        [jnp.where(mine - j * per == lane, rr, 0.0).astype(BF16) for j in range(OCTET // per)],
        axis=1,
    )


def mix_chunk(c, chunks, cond, reset_at, tokens, attended, steps, embed, gain, w_out, w_in, carry):
    frames_all, res, width = tokens.shape
    heads = steps.shape[-1]
    peers = len(attended)
    part_frames = attended[0].shape[0]
    frames = part_frames * peers
    tiles = frames // TILE_FRAMES
    rows = TILE_FRAMES * res
    half = TILE_FRAMES * OCTET
    mixed_width = w_in.shape[1]
    state = (mixed_width - 2 * width) // 2
    spread = res * state
    last = c == chunks - 1
    per_pay = res // (GROUP * HALVES)
    pay_rows = per_pay * state
    carry_args = [] if carry is None else list(carry)
    n_in = 8 + peers

    def body(*refs):
        cond_ref, reset_ref, tok_ref = refs[:3]
        att_refs = refs[3 : 3 + peers]
        steps_ref, embed_ref, gain_ref, wo_ref, wi_ref = refs[3 + peers : n_in]
        pos = n_in + len(carry_args)
        carry_refs = refs[n_in:pos]
        mid_ref, mixed_ref, entry_ref, reach_ref = refs[pos : pos + 4]
        pos += 4
        pay_refs = refs[pos : pos + GROUP * HALVES] if last else ()
        pos += len(pay_refs)
        if last:
            att_s, s_ref, p_ref, p_wide = refs[pos:]
        else:
            s_ref, p_ref, att_s = refs[pos:]
        reset = reset_ref[0]
        me, place = lax.axis_index("res"), my_place()
        for k in range(peers):
            att_s[me ^ k] = att_refs[k][...]
        if carry is None:
            s_ref[...] = jnp.zeros_like(s_ref)
            p_ref[...] = jnp.ones_like(p_ref)
        else:
            s_ref[...] = carry_refs[0][...]
            p_ref[...] = carry_refs[1][...]
        embed_row = joined_row(embed_ref)
        gain_row = joined_row(gain_ref)
        att_all = att_s[...].reshape(frames * res, width)
        for i in range(tiles):
            g0 = c * frames + i * TILE_FRAMES
            g_end = g0 + TILE_FRAMES - 1
            sl = slice(i * rows, (i + 1) * rows)
            hidden = jnp.concatenate(
                [
                    tok_ref[i * TILE_FRAMES + f].astype(F32)
                    + cond_ref[g0 + f].astype(F32) * embed_row
                    for f in range(TILE_FRAMES)
                ],
                axis=0,
            )
            mid = hidden + nn_dot(att_all[sl], wo_ref[...])
            mid_ref[sl] = mid
            mixer_in = rms_rows(mid, gain_row)
            mixer_in = jnp.concatenate(octets(mixer_in, TILE_FRAMES, res), axis=0).astype(BF16)
            mixed_ref[sl, 2 * width :] = nn_dot(mixer_in, wi_ref[:, 2 * width :]).astype(BF16)
            mixed_ref[sl, width : 2 * width] = nn_dot(
                mixer_in, wi_ref[:, width : 2 * width]
            ).astype(BF16)
            mixed_ref[sl, :width] = nn_dot(mixer_in, wi_ref[:, :width]).astype(BF16)
            tile_steps = steps_ref[i * TILE_FRAMES : (i + 1) * TILE_FRAMES]
            keep_end = [
                jnp.where((reset > g0 + f) & (reset <= g_end), 0.0, 1.0).astype(F32)
                for f in range(TILE_FRAMES)
            ]
            keep_all = jnp.where((reset >= g0) & (reset <= g_end), 0.0, 1.0).astype(F32)
            entry_ref[i] = s_ref[...].astype(BF16)
            reach_ref[i] = p_ref[...]
            for o in range(res // OCTET):
                os = slice(i * rows + o * half, i * rows + (o + 1) * half)
                st = tile_steps[:, o * OCTET : (o + 1) * OCTET].reshape(half, heads)
                decay = wide_decays(st, heads, width)
                after = [jnp.ones((OCTET, width), F32)]
                for f in range(TILE_FRAMES - 1, 0, -1):
                    after.append(after[-1] * frame_rows(decay, f))
                transit = after[-1] * frame_rows(decay, 0) * keep_all
                after = after[::-1]
                kept = jnp.concatenate([a * s for a, s in zip(after, keep_end)], axis=0)
                inner = mixed_ref[os, width : 2 * width].astype(F32)
                kept = (inner * kept).astype(BF16)
                maps = mixed_ref[os, 2 * width :].astype(F32)
                write_t = maps.T[:state]
                col = lax.broadcasted_iota(jnp.int32, (state, half), 1) % OCTET
                write = jnp.concatenate(
                    [jnp.where(col == r, write_t, 0.0).astype(BF16) for r in range(OCTET)], axis=0
                )
                added = nn_dot(write, kept)
                for r in range(OCTET):
                    rs = slice(r * state, (r + 1) * state)
                    ss = slice((o * OCTET + r) * state, (o * OCTET + r + 1) * state)
                    s_ref[ss] = s_ref[ss] * transit[r : r + 1] + added[rs]
                po = slice(o * OCTET, (o + 1) * OCTET)
                p_ref[po] = p_ref[po] * transit
        if not last:
            return
        p_all = p_ref[...]
        for r in range(res):
            p_wide[r] = jnp.broadcast_to(p_all[r : r + 1], (8, width))
        sub = lax.broadcasted_iota(jnp.int32, (CARRY_ROWS, width), 0) % 8
        for e in range(HALVES):
            for k in range(GROUP):
                r0 = ((place ^ k) * HALVES + e) * per_pay
                out = pay_refs[e * GROUP + k]
                start = pl.multiple_of(r0 * state, pay_rows)
                out[:pay_rows] = s_ref[pl.ds(start, pay_rows), :].astype(BF16)
                for n in range(0, per_pay, 2):
                    value = jnp.concatenate([p_wide[r0 + n], p_wide[r0 + n + 1]], axis=0)
                    upper = value.astype(BF16).astype(F32)
                    lo = pay_rows + n * 8
                    out[lo : lo + 16] = jnp.where(sub < 4, upper, value - upper).astype(BF16)

    chunk_rows = frames * res
    in_specs = (
        [SMEM_SPEC, SMEM_SPEC]
        + [pl.BlockSpec((frames, res, width), lambda i: (c, 0, 0))]
        + [whole(attended[0].shape)] * peers
        + [pl.BlockSpec((frames, res, heads), lambda i: (c, 0, 0))]
        + [whole(a.shape) for a in (embed, gain, w_out, w_in)]
        + [whole(a.shape) for a in carry_args]
    )
    out_shape = [
        jax.ShapeDtypeStruct((chunk_rows, width), F32),
        jax.ShapeDtypeStruct((chunk_rows, mixed_width), BF16),
        jax.ShapeDtypeStruct((tiles, spread, width), BF16),
        jax.ShapeDtypeStruct((tiles, res, width), F32),
    ]
    scratch = [pltpu.VMEM((peers, part_frames, res, width), BF16)]
    if last:
        pay = (pay_rows + 8 * per_pay, width)
        out_shape += [jax.ShapeDtypeStruct(pay, BF16)] * (GROUP * HALVES)
        scratch += [
            pltpu.VMEM((spread, width), F32),
            pltpu.VMEM((res, width), F32),
            pltpu.VMEM((res, 8, width), F32),
        ]
    else:
        out_shape += [
            jax.ShapeDtypeStruct((spread, width), F32),
            jax.ShapeDtypeStruct((res, width), F32),
        ]
    outs = pl.pallas_call(
        body,
        grid=(1,),
        in_specs=in_specs,
        out_specs=[whole(o.shape) for o in out_shape],
        out_shape=out_shape,
        scratch_shapes=scratch,
        compiler_params=grant(20),
        name="mix",
    )(cond, reset_at, tokens, *attended, steps, embed, gain, w_out, w_in, *carry_args)
    return outs[:4], outs[4:]


def scan_chunk(c, reset_at, skip, steps, mixed, entry, reach, mixer_scale):
    tiles, spread, width = entry.shape
    _, res, heads = steps.shape
    state = spread // res
    rows = TILE_FRAMES * res
    half = TILE_FRAMES * OCTET
    octet_state = OCTET * state

    def body(
        reset_ref, skip_ref, steps_ref, mixed_ref, entry_ref, reach_ref, z_ref, ag_ref, rr_ref
    ):
        reset = reset_ref[0]
        feature = lax.broadcasted_iota(jnp.int32, (1, width), 1) // (width // heads)
        skip_row = jnp.zeros((1, width), F32)
        for h in range(heads):
            skip_row = jnp.where(feature == h, skip_ref[h], skip_row)
        g0 = c * tiles * TILE_FRAMES + pl.program_id(0) * TILE_FRAMES
        row_i = lax.broadcasted_iota(jnp.int32, (half, half), 0)
        col_i = lax.broadcasted_iota(jnp.int32, (half, half), 1)
        edge = (reset - g0) * OCTET
        joined = (
            ((row_i % OCTET) == (col_i % OCTET))
            & (row_i >= col_i)
            & ((row_i >= edge) == (col_i >= edge))
        )
        keep_start = [
            jnp.where((reset >= g0) & (reset <= g0 + f), 0.0, 1.0).astype(F32)
            for f in range(TILE_FRAMES)
        ]
        for o in range(res // OCTET):
            os = slice(o * half, (o + 1) * half)
            st = steps_ref[:, o * OCTET : (o + 1) * OCTET].reshape(half, heads)
            decay = wide_decays(st, heads, width)
            before = [frame_rows(decay, 0)]
            for f in range(1, TILE_FRAMES):
                before.append(before[-1] * frame_rows(decay, f))
            after = [jnp.ones((OCTET, width), F32)]
            for f in range(TILE_FRAMES - 1, 0, -1):
                after.append(after[-1] * frame_rows(decay, f))
            after = jnp.concatenate(after[::-1], axis=0)
            back = 1.0 / before[-1]
            relative = jnp.concatenate([b * back for b in before], axis=0)
            from_base = jnp.concatenate([b * s for b, s in zip(before, keep_start)], axis=0)
            inner = mixed_ref[os, width : 2 * width].astype(F32)
            ww, rr = twice_each(mixed_ref[os, 2 * width :].astype(F32), state)
            rr_ref[os] = rr.astype(BF16)
            gram = nt_dot(rr.astype(BF16), ww.astype(BF16)) * 0.5
            gram = jnp.where(joined, gram, 0.0).astype(BF16)
            near = nn_dot(gram, (inner * after).astype(BF16)) * relative
            entry_o = entry_ref[0, o * octet_state : (o + 1) * octet_state]
            far = nn_dot(spread_read(rr, state), entry_o) * from_base
            gate = mixed_ref[os, :width].astype(F32)
            silu = gate / (1.0 + jnp.exp(-gate))
            z_ref[os] = ((near + far) * mixer_scale + skip_row * inner) * silu
            start = reach_ref[0, o * OCTET : (o + 1) * OCTET] * mixer_scale
            reached = jnp.concatenate(
                [start * frame_rows(from_base, f) for f in range(TILE_FRAMES)], axis=0
            )
            ag_ref[os] = (reached * silu).astype(BF16)

    total = tiles * rows

    def row_block(cols):
        return pl.BlockSpec((rows, cols), lambda i: (i, 0))

    return pl.pallas_call(
        body,
        grid=(tiles,),
        in_specs=[
            SMEM_SPEC,
            SMEM_SPEC,
            pl.BlockSpec((TILE_FRAMES, res, heads), lambda i: (c * tiles + i, 0, 0)),
            row_block(mixed.shape[1]),
            pl.BlockSpec((1, spread, width), lambda i: (i, 0, 0)),
            pl.BlockSpec((1, res, width), lambda i: (i, 0, 0)),
        ],
        out_specs=[row_block(width), row_block(width), row_block(LANES)],
        out_shape=[
            jax.ShapeDtypeStruct((total, width), F32),
            jax.ShapeDtypeStruct((total, width), BF16),
            jax.ShapeDtypeStruct((total, LANES), BF16),
        ],
        compiler_params=grant(14),
        name="scan",
    )(reset_at, skip, steps, mixed, entry, reach)


def decay_rows(tail, n):
    tail = tail.astype(F32)
    return [tail[8 * i : 8 * i + 1] + tail[8 * i + 4 : 8 * i + 5] for i in range(n)]


def residues_of(pay, state):
    return pay // (state + 8)


def group_total(got, after, state):
    pay, width = got[0].shape
    n = residues_of(pay, state)
    body_rows = n * state

    def body(*refs):
        got_refs = refs[:GROUP]
        out_ref, sorted_s = refs[-2:]
        place = my_place()
        for k in range(GROUP):
            sorted_s[place ^ k] = got_refs[k][...]
        tails = [decay_rows(sorted_s[j, body_rows:], n) for j in range(GROUP)]
        sub = lax.broadcasted_iota(jnp.int32, (CARRY_ROWS, width), 0) % 8
        lines = []
        for i in range(n):
            rs = slice(i * state, (i + 1) * state)
            total = sorted_s[0, rs].astype(F32)
            product = tails[0][i]
            for j in range(1, GROUP):
                total = total * tails[j][i] + sorted_s[j, rs].astype(F32)
                product = product * tails[j][i]
            out_ref[rs] = total.astype(BF16)
            lines.append(jnp.broadcast_to(product, (8, width)))
        for i in range(0, n, 2):
            value = jnp.concatenate(lines[i : i + 2], axis=0)
            upper = value.astype(BF16).astype(F32)
            lo = body_rows + 8 * i
            out_ref[lo : lo + 16] = jnp.where(sub < 4, upper, value - upper).astype(BF16)

    return pl.pallas_call(
        body,
        grid=(1,),
        in_specs=[whole((pay, width))] * GROUP + [HBM_SPEC] * len(after),
        out_specs=whole((pay, width)),
        out_shape=jax.ShapeDtypeStruct((pay, width), BF16),
        scratch_shapes=[pltpu.VMEM((GROUP, pay, width), BF16)],
        compiler_params=grant(6),
        name="group_total",
    )(*got, *after)


def group_prefixes(got, entering, after, state):
    pay, width = got[0].shape
    n = residues_of(pay, state)
    body_rows = n * state

    def body(*refs):
        got_refs, in_ref = refs[:GROUP], refs[GROUP]
        out_refs = refs[-GROUP - 2 : -2]
        sorted_s, prefix_s = refs[-2:]
        place = my_place()
        for k in range(GROUP):
            sorted_s[place ^ k] = got_refs[k][...]
        tails = [decay_rows(sorted_s[j, body_rows:], n) for j in range(GROUP)]
        for i in range(n):
            rs = slice(i * state, (i + 1) * state)
            total = in_ref[rs].astype(F32)
            prefix_s[0, rs] = total.astype(BF16)
            for j in range(GROUP - 1):
                total = total * tails[j][i] + sorted_s[j, rs].astype(F32)
                prefix_s[j + 1, rs] = total.astype(BF16)
        for k in range(GROUP):
            out_refs[k][...] = prefix_s[place ^ k]

    spec = whole((pay, width))
    out = whole((body_rows, width))
    return pl.pallas_call(
        body,
        grid=(1,),
        in_specs=[spec] * (GROUP + 1) + [HBM_SPEC] * len(after),
        out_specs=[out] * GROUP,
        out_shape=[jax.ShapeDtypeStruct((body_rows, width), BF16)] * GROUP,
        scratch_shapes=[
            pltpu.VMEM((GROUP, pay, width), BF16),
            pltpu.VMEM((GROUP, body_rows, width), BF16),
        ],
        compiler_params=grant(8),
        name="group_prefixes",
    )(*got, entering, *after)


def join_payloads(earlier, later, state):
    n = residues_of(later.shape[0], state)
    body_rows = n * state
    width = later.shape[1]
    early = decay_rows(earlier[body_rows:], n)
    late = decay_rows(later[body_rows:], n)
    parts, lines = [], []
    for i in range(n):
        rs = slice(i * state, (i + 1) * state)
        parts.append(earlier[rs].astype(F32) * late[i] + later[rs].astype(F32))
        value = early[i] * late[i]
        upper = value.astype(BF16).astype(F32)
        lines += [jnp.broadcast_to(upper, (4, width)), jnp.broadcast_to(value - upper, (4, width))]
    return jnp.concatenate(parts + lines, axis=0).astype(BF16)


def states_entering(payloads, covers, state, tm_size):
    groups = tm_size // GROUP
    order = list(range(GROUP - 1, 0, -1))

    def swap(parts):
        moved = {
            k: lax.ppermute(parts[k], "tm", [(i, i ^ k) for i in range(tm_size)]) for k in order
        }
        return [parts[0]] + [moved[k] for k in range(1, GROUP)]

    def onward(value, hops):
        moved = hops * GROUP
        return lax.ppermute(value, "tm", [(i, i + moved) for i in range(tm_size - moved)])

    gathered = [swap(payloads[e * GROUP : (e + 1) * GROUP]) for e in range(HALVES)]
    result = []
    for e, got in enumerate(gathered):
        total = group_total(got, [] if e else covers[:1], state)
        entering = onward(total, 1) if groups > 1 else jnp.zeros_like(total)
        hops = 1
        while hops < groups - 1:
            entering = join_payloads(onward(entering, hops), entering, state)
            hops *= 2
        result += swap(group_prefixes(got, entering, [] if e else covers[1:], state))
    return result


def finish_chunk(c, entered, mid, z, ag, rr, w_mix, frames, res, state, done):
    total, width = mid.shape
    rows = TILE_FRAMES * res
    half = TILE_FRAMES * OCTET
    tiles = total // rows
    piece = entered[0].shape[0]
    spread = res * state
    octet_state = OCTET * state
    done_args = [] if done is None else [done]

    def body(*refs):
        n = GROUP * HALVES
        in_refs = refs[:n]
        mid_ref, z_ref, ag_ref, rr_ref, w_ref = refs[n : n + 5]
        out_ref, state_s = refs[-2:]

        @pl.when(pl.program_id(0) == 0)
        def _():
            place = my_place()
            for e in range(HALVES):
                for k in range(GROUP):
                    state_s[(place ^ k) * HALVES + e] = in_refs[e * GROUP + k][...]

        states = state_s[...].reshape(spread, width)
        cubes = []
        for o in range(res // OCTET):
            os = slice(o * half, (o + 1) * half)
            read = spread_read(rr_ref[os].astype(F32), state)
            far = nn_dot(read, states[o * octet_state : (o + 1) * octet_state])
            gated = z_ref[os] + ag_ref[os].astype(F32) * far
            cubes.append(gated.reshape(TILE_FRAMES, OCTET, width))
        gated = jnp.concatenate(cubes, axis=1).reshape(rows, width).astype(BF16)
        out = mid_ref[...] + nn_dot(gated, w_ref[...])
        out_ref[...] = out.astype(BF16).reshape(TILE_FRAMES, res, width)

    def tile_spec(cols):
        return pl.BlockSpec((rows, cols), lambda i: (i, 0))

    n_in = GROUP * HALVES + 5
    return pl.pallas_call(
        body,
        grid=(tiles,),
        in_specs=[whole((piece, width))] * (GROUP * HALVES)
        + [tile_spec(width), tile_spec(width), tile_spec(width), tile_spec(LANES)]
        + [whole(w_mix.shape)]
        + [HBM_SPEC] * len(done_args),
        out_specs=pl.BlockSpec((TILE_FRAMES, res, width), lambda i: (c * tiles + i, 0, 0)),
        out_shape=jax.ShapeDtypeStruct((frames, res, width), BF16),
        scratch_shapes=[pltpu.VMEM((GROUP * HALVES, piece, width), BF16)],
        input_output_aliases={n_in: 0} if done_args else {},
        compiler_params=grant(14),
        name="finish",
    )(*entered, mid, z, ag, rr, w_mix, *done_args)


def local(
    tokens,
    cond_mask,
    cond_embed,
    attn_gain,
    w_qkv,
    w_out,
    mix_gain,
    w_in,
    decay_steps,
    segment_ids,
    skip_gain,
    w_mix_out,
):
    frames, res, width = tokens.shape
    heads = skip_gain.shape[0]
    state = (w_in.shape[1] - 2 * width) // 2
    tm_size = lax.axis_size("tm")
    peers = lax.axis_size("res")
    part = PART_FRAMES
    chunks = frames // (part * peers)
    order = list(range(peers - 1, 0, -1))

    def swap(value, k):
        return lax.ppermute(value, "res", [(i, i ^ k) for i in range(peers)])

    ids = segment_ids.reshape(-1, LANES)
    reset_at, pieces = prepare(tokens, ids, [], chunks, peers)
    gathered = []
    for c in range(chunks):
        mine = pieces[c * peers : (c + 1) * peers]
        got = {k: swap(mine[k], k) for k in order}
        got[0] = mine[0]
        gathered.append([got[k] for k in range(peers)])

    embed = cond_embed.reshape(-1, LANES)
    first_gain = attn_gain.reshape(-1, LANES)
    second_gain = mix_gain.reshape(-1, LANES)
    mixer_scale = 1.0 / math.sqrt(frames * tm_size * state)

    attended = []
    for c in range(chunks):
        outs = attend_chunk(
            cond_mask, gathered[c], embed, first_gain, w_qkv, c * part * peers, heads
        )
        back = {k: swap(outs[k], k) for k in order}
        back[0] = outs[0]
        attended.append([back[k] for k in range(peers)])

    carry, held = None, []
    for c in range(chunks):
        out, carry = mix_chunk(
            c,
            chunks,
            cond_mask,
            reset_at,
            tokens,
            attended[c],
            decay_steps,
            embed,
            second_gain,
            w_out,
            w_in,
            carry,
        )
        held.append(out)
    scanned = [
        scan_chunk(c, reset_at, skip_gain, decay_steps, mixed, entry, reach, mixer_scale)
        for c, (_, mixed, entry, reach) in enumerate(held)
    ]
    covers = [rr for _, _, rr in scanned]
    entered = states_entering(carry, covers, state, tm_size)
    done = None
    for c, (z, ag, rr) in enumerate(scanned):
        mid = held[c][0]
        done = finish_chunk(
            c, entered, mid, z, ag, rr, w_mix_out, frames, res, state, done
        )
    return done


def solution(mesh):
    in_specs = (
        P("tm", "res", None),
        P("tm"),
        P(),
        P(),
        P(),
        P(),
        P(),
        P(),
        P("tm", "res", None),
        P(),
        P(),
        P(),
    )
    out_specs = P("tm", "res", None)
    return jax.shard_map(local, mesh=mesh, in_specs=in_specs, out_specs=out_specs, check_vma=False)
```

```python
import math

import jax
import jax.numpy as jnp
from jax import lax
from jax.experimental import pallas as pl
from jax.experimental.pallas import tpu as pltpu
from jax.sharding import PartitionSpec as P


BF16 = jnp.bfloat16
F32 = jnp.float32
LANES = 128
PART_FRAMES = 16
STAGE_FRAMES = 4
TILE_FRAMES = 32
OCTET = 8
GROUP = 4
CARRY_ROWS = 16


def rms_rows(rows, gain):
    mean = jnp.mean(rows * rows, axis=-1, keepdims=True)
    return rows * lax.rsqrt(mean + 1e-06) * gain


def nt_dot(a, b):
    return lax.dot_general(a, b, (((1,), (1,)), ((), ())), preferred_element_type=F32)


def tn_dot(a, b):
    return lax.dot_general(a, b, (((0,), (0,)), ((), ())), preferred_element_type=F32)


def nn_dot(a, b):
    return jnp.dot(a, b, preferred_element_type=F32)


def joined_row(ref):
    return jnp.concatenate([ref[i : i + 1] for i in range(ref.shape[0])], axis=1)


def first_reset(ids_ref, frames):
    ids = ids_ref[...]
    first = (ids == jnp.min(ids)).astype(F32)
    return jnp.sum(first).astype(jnp.int32) - lax.axis_index("tm") * frames


def my_place():
    return lax.axis_index("tm") % GROUP


def whole(shape):
    return pl.BlockSpec(shape, lambda i: (0,) * len(shape))


def grant(mib):
    return pltpu.CompilerParams(vmem_limit_bytes=mib << 20)


SMEM_SPEC = pl.BlockSpec(memory_space=pltpu.SMEM)
HBM_SPEC = pl.BlockSpec(memory_space=pl.ANY)


def prepare(tokens, after, chunks, peers):
    frames, res, width = tokens.shape
    part = frames // (chunks * peers)
    count = chunks * peers

    def body(*refs):
        tok_ref, out_refs = refs[0], refs[-count:]
        me = lax.axis_index("res")
        for c in range(chunks):
            for k in range(peers):
                start = c * part * peers + (me ^ k) * part
                out_refs[c * peers + k][...] = tok_ref[pl.ds(start, part)]

    piece = (part, res, width)
    return pl.pallas_call(
        body,
        grid=(1,),
        in_specs=[whole(tokens.shape)] + [HBM_SPEC] * len(after),
        out_specs=[whole(piece)] * count,
        out_shape=[jax.ShapeDtypeStruct(piece, tokens.dtype)] * count,
        compiler_params=grant(10),
        name="prepare",
    )(tokens, *after)


def attend_chunk(cond, parts, embed, gain, w_qkv, first_frame, heads, follow):
    peers = len(parts)
    frames, res, width = parts[0].shape
    head_size = width // heads
    keys = peers * res
    pairs = width // LANES
    inv_root = 1.0 / math.sqrt(head_size)

    def body(cond_ref, *refs):
        tok_refs = refs[:peers]
        embed_ref, gain_ref, w_ref = refs[peers : peers + 3]
        out_refs = refs[-peers - 2 : -2]
        norm_s, qkv_s = refs[-2:]
        me = lax.axis_index("res")
        embed_row = joined_row(embed_ref)
        gain_row = joined_row(gain_ref)
        for f in range(frames):
            flag = cond_ref[first_frame + me * frames + f].astype(F32)
            added = flag * embed_row
            for k in range(peers):
                rows = tok_refs[k][f].astype(F32) + added
                norm_s[k, f] = rms_rows(rows, gain_row).astype(BF16)
        flat = norm_s[...].reshape(peers * frames * res, width)
        shape = (peers, frames, res)
        got = nn_dot(flat, w_ref[:, : 2 * width]).astype(BF16)
        scaled = got[:, :width] * jnp.asarray(inv_root, BF16)
        qkv_s[:, :, :, :width] = scaled.reshape(*shape, width)
        qkv_s[:, :, :, width : 2 * width] = got[:, width:].reshape(*shape, width)
        got = nn_dot(flat, w_ref[:, 2 * width :]).astype(BF16)
        qkv_s[:, :, :, 2 * width :] = got.reshape(*shape, width)
        lane = lax.broadcasted_iota(jnp.int32, (1, LANES), 1)
        first = (lane < head_size).astype(BF16)
        second = (lane >= head_size).astype(BF16)
        pick = lax.broadcasted_iota(jnp.int32, (keys, LANES), 1) < head_size

        def stage(f0):
            units = [(f0 + f, p) for f in range(STAGE_FRAMES) for p in range(pairs)]

            def part(n, f, p):
                lo = n * width + p * LANES
                return qkv_s[:, pl.ds(f, 1), :, lo : lo + LANES].reshape(keys, LANES)

            scores = []
            for f, p in units:
                q = part(0, f, p)
                stacked = jnp.concatenate([q * first, q * second], axis=0)
                scores.append(nt_dot(part(1, f, p), stacked))
            tops = [jnp.max(x, axis=0, keepdims=True) for x in scores]
            weights = [jnp.exp(x - t) for x, t in zip(scores, tops)]
            totals = [jnp.sum(w, axis=0, keepdims=True) for w in weights]
            weights = [(w * (1.0 / t)).astype(BF16) for w, t in zip(weights, totals)]
            both = [tn_dot(w, part(2, f, p)) for w, (f, p) in zip(weights, units)]
            for got, (f, p) in zip(both, units):
                att = jnp.where(pick, got[:keys], got[keys:]).astype(BF16)
                for k in range(peers):
                    out_refs[k][pl.ds(f, 1), :, p * LANES : (p + 1) * LANES] = att[
                        k * res : (k + 1) * res
                    ].reshape(1, res, LANES)

        def step(i, _):
            stage(i * STAGE_FRAMES)
            return 0

        lax.fori_loop(0, frames // STAGE_FRAMES, step, 0)

    block = whole((frames, res, width))
    return pl.pallas_call(
        body,
        grid=(1,),
        in_specs=[SMEM_SPEC]
        + [block] * peers
        + [whole(a.shape) for a in (embed, gain, w_qkv)]
        + [HBM_SPEC] * len(follow),
        out_specs=[block] * peers,
        out_shape=[jax.ShapeDtypeStruct((frames, res, width), BF16)] * peers,
        scratch_shapes=[
            pltpu.VMEM((peers, frames, res, width), BF16),
            pltpu.VMEM((peers, frames, res, 3 * width), BF16),
        ],
        compiler_params=grant(14),
        name="attend",
    )(cond, *parts, embed, gain, w_qkv, *follow)


def octets(rows, frames, res):
    n = rows.shape[-1]
    cube = rows.reshape(frames, res, n)
    return [
        cube[:, o * OCTET : (o + 1) * OCTET].reshape(frames * OCTET, n) for o in range(res // OCTET)
    ]


def wide_decays(steps, heads, width):
    values = 1.0 - steps.astype(F32) * (1.0 / 4096.0)
    rows = values.shape[0]
    head_size = width // heads
    per = LANES // head_size
    lane_head = lax.broadcasted_iota(jnp.int32, (rows, LANES), 1) // head_size
    parts = []
    for p in range(width // LANES):
        part = jnp.broadcast_to(values[:, p * per : p * per + 1], (rows, LANES))
        for h in range(1, per):
            col = values[:, p * per + h : p * per + h + 1]
            part = jnp.where(lane_head == h, jnp.broadcast_to(col, (rows, LANES)), part)
        parts.append(part)
    return jnp.concatenate(parts, axis=1)


def frame_rows(value, f):
    return value[f * OCTET : (f + 1) * OCTET]


def twice_each(maps, state):
    low = lax.broadcasted_iota(jnp.int32, maps.shape, 1) < state
    turned = pltpu.roll(maps, state, 1)
    return jnp.where(low, maps, turned), jnp.where(low, turned, maps)


def spread_read(rr, state):
    rows = rr.shape[0]
    mine = lax.broadcasted_iota(jnp.int32, (rows, LANES), 0) % OCTET
    lane = lax.broadcasted_iota(jnp.int32, (rows, LANES), 1) // state
    per = LANES // state
    return jnp.concatenate(
        [jnp.where(mine - j * per == lane, rr, 0.0).astype(BF16) for j in range(OCTET // per)],
        axis=1,
    )


def mix_chunk(c, chunks, cond, ids, tokens, attended, steps, embed, gain, w_out, w_in, carry, follow):
    frames_all, res, width = tokens.shape
    heads = steps.shape[-1]
    peers = len(attended)
    part_frames = attended[0].shape[0]
    frames = part_frames * peers
    tiles = frames // TILE_FRAMES
    rows = TILE_FRAMES * res
    half = TILE_FRAMES * OCTET
    mixed_width = w_in.shape[1]
    state = (mixed_width - 2 * width) // 2
    spread = res * state
    last = c == chunks - 1
    pays = GROUP * (res // OCTET)
    per_pay = OCTET // GROUP
    pay_rows = per_pay * state
    carry_args = [] if carry is None else list(carry)
    n_in = 8 + peers

    def body(*refs):
        cond_ref, ids_ref, tok_ref = refs[:3]
        att_refs = refs[3 : 3 + peers]
        steps_ref, embed_ref, gain_ref, wo_ref, wi_ref = refs[3 + peers : n_in]
        pos = n_in + len(carry_args)
        carry_refs = refs[n_in:pos]
        pos += len(follow)
        mid_ref, mixed_ref, entry_ref, reach_ref = refs[pos : pos + 4]
        pos += 4
        pay_refs = refs[pos : pos + pays] if last else ()
        pos += len(pay_refs)
        if last:
            att_s, s_ref, p_ref, p_wide = refs[pos:]
        else:
            s_ref, p_ref, att_s = refs[pos:]
        reset = first_reset(ids_ref, frames_all)
        me, place = lax.axis_index("res"), my_place()
        for k in range(peers):
            att_s[me ^ k] = att_refs[k][...]
        if carry is None:
            s_ref[...] = jnp.zeros_like(s_ref)
            p_ref[...] = jnp.ones_like(p_ref)
        else:
            s_ref[...] = carry_refs[0][...]
            p_ref[...] = carry_refs[1][...]
        embed_row = joined_row(embed_ref)
        gain_row = joined_row(gain_ref)
        att_all = att_s[...].reshape(frames * res, width)
        for i in range(tiles):
            g0 = c * frames + i * TILE_FRAMES
            g_end = g0 + TILE_FRAMES - 1
            sl = slice(i * rows, (i + 1) * rows)
            hidden = jnp.concatenate(
                [
                    tok_ref[i * TILE_FRAMES + f].astype(F32)
                    + cond_ref[g0 + f].astype(F32) * embed_row
                    for f in range(TILE_FRAMES)
                ],
                axis=0,
            )
            mid = hidden + nn_dot(att_all[sl], wo_ref[...])
            mid_ref[sl] = jnp.concatenate(octets(mid, TILE_FRAMES, res), axis=0)
            mixer_in = rms_rows(mid, gain_row)
            mixer_in = jnp.concatenate(octets(mixer_in, TILE_FRAMES, res), axis=0).astype(BF16)
            mixed_ref[sl, width:] = nn_dot(mixer_in, wi_ref[:, width:]).astype(BF16)
            mixed_ref[sl, :width] = nn_dot(mixer_in, wi_ref[:, :width]).astype(BF16)
            tile_steps = steps_ref[i * TILE_FRAMES : (i + 1) * TILE_FRAMES]
            keep_end = [
                jnp.where((reset > g0 + f) & (reset <= g_end), 0.0, 1.0).astype(F32)
                for f in range(TILE_FRAMES)
            ]
            keep_all = jnp.where((reset >= g0) & (reset <= g_end), 0.0, 1.0).astype(F32)
            entry_ref[i] = s_ref[...].astype(BF16)
            reach_ref[i] = p_ref[...]
            for o in range(res // OCTET):
                os = slice(i * rows + o * half, i * rows + (o + 1) * half)
                st = tile_steps[:, o * OCTET : (o + 1) * OCTET].reshape(half, heads)
                decay = wide_decays(st, heads, width)
                after = [jnp.ones((OCTET, width), F32)]
                for f in range(TILE_FRAMES - 1, 0, -1):
                    after.append(after[-1] * frame_rows(decay, f))
                transit = after[-1] * frame_rows(decay, 0) * keep_all
                after = after[::-1]
                kept = jnp.concatenate([a * s for a, s in zip(after, keep_end)], axis=0)
                inner = mixed_ref[os, width : 2 * width].astype(F32)
                kept = (inner * kept).astype(BF16)
                maps = mixed_ref[os, 2 * width :].astype(F32)
                write_t = maps.T[:state]
                col = lax.broadcasted_iota(jnp.int32, (state, half), 1) % OCTET
                write = jnp.concatenate(
                    [jnp.where(col == r, write_t, 0.0).astype(BF16) for r in range(OCTET)], axis=0
                )
                added = nn_dot(write, kept)
                for r in range(OCTET):
                    rs = slice(r * state, (r + 1) * state)
                    ss = slice((o * OCTET + r) * state, (o * OCTET + r + 1) * state)
                    s_ref[ss] = s_ref[ss] * transit[r : r + 1] + added[rs]
                po = slice(o * OCTET, (o + 1) * OCTET)
                p_ref[po] = p_ref[po] * transit
        if not last:
            return
        p_all = p_ref[...]
        for r in range(res):
            p_wide[r] = jnp.broadcast_to(p_all[r : r + 1], (8, width))
        sub = lax.broadcasted_iota(jnp.int32, (CARRY_ROWS, width), 0) % 8
        for e in range(res // OCTET):
            for k in range(GROUP):
                r0 = e * OCTET + (place ^ k) * per_pay
                out = pay_refs[e * GROUP + k]
                start = pl.multiple_of(r0 * state, pay_rows)
                out[:pay_rows] = s_ref[pl.ds(start, pay_rows), :].astype(BF16)
                for n in range(0, per_pay, 2):
                    value = jnp.concatenate([p_wide[r0 + n], p_wide[r0 + n + 1]], axis=0)
                    upper = value.astype(BF16).astype(F32)
                    lo = pay_rows + n * 8
                    out[lo : lo + 16] = jnp.where(sub < 4, upper, value - upper).astype(BF16)

    chunk_rows = frames * res
    in_specs = (
        [SMEM_SPEC, whole(ids.shape)]
        + [pl.BlockSpec((frames, res, width), lambda i: (c, 0, 0))]
        + [whole(attended[0].shape)] * peers
        + [pl.BlockSpec((frames, res, heads), lambda i: (c, 0, 0))]
        + [whole(a.shape) for a in (embed, gain, w_out, w_in)]
        + [whole(a.shape) for a in carry_args]
        + [HBM_SPEC] * len(follow)
    )
    out_shape = [
        jax.ShapeDtypeStruct((chunk_rows, width), F32),
        jax.ShapeDtypeStruct((chunk_rows, mixed_width), BF16),
        jax.ShapeDtypeStruct((tiles, spread, width), BF16),
        jax.ShapeDtypeStruct((tiles, res, width), F32),
    ]
    scratch = [pltpu.VMEM((peers, part_frames, res, width), BF16)]
    if last:
        pay = (pay_rows + 8 * per_pay, width)
        out_shape += [jax.ShapeDtypeStruct(pay, BF16)] * pays
        scratch += [
            pltpu.VMEM((spread, width), F32),
            pltpu.VMEM((res, width), F32),
            pltpu.VMEM((res, 8, width), F32),
        ]
    else:
        out_shape += [
            jax.ShapeDtypeStruct((spread, width), F32),
            jax.ShapeDtypeStruct((res, width), F32),
        ]
    outs = pl.pallas_call(
        body,
        grid=(1,),
        in_specs=in_specs,
        out_specs=[whole(o.shape) for o in out_shape],
        out_shape=out_shape,
        scratch_shapes=scratch,
        compiler_params=grant(20),
        name="mix",
    )(cond, ids, tokens, *attended, steps, embed, gain, w_out, w_in, *carry_args, *follow)
    return outs[:4], outs[4:]


def scan_octet(o, c, frames_all, ids, skip, steps, mixed, entry, reach, mixer_scale):
    tiles, spread, width = entry.shape
    _, res, heads = steps.shape
    state = spread // res
    half = TILE_FRAMES * OCTET
    octet_state = OCTET * state
    octet_count = res // OCTET

    def body(
        ids_ref, skip_ref, steps_ref, mixed_ref, entry_ref, reach_ref, z_ref, ag_ref, rr_ref
    ):
        reset = first_reset(ids_ref, frames_all)
        feature = lax.broadcasted_iota(jnp.int32, (1, width), 1) // (width // heads)
        skip_row = jnp.zeros((1, width), F32)
        for h in range(heads):
            skip_row = jnp.where(feature == h, skip_ref[h], skip_row)
        g0 = c * tiles * TILE_FRAMES + pl.program_id(0) * TILE_FRAMES
        row_i = lax.broadcasted_iota(jnp.int32, (half, half), 0)
        col_i = lax.broadcasted_iota(jnp.int32, (half, half), 1)
        edge = (reset - g0) * OCTET
        joined = (
            ((row_i % OCTET) == (col_i % OCTET))
            & (row_i >= col_i)
            & ((row_i >= edge) == (col_i >= edge))
        )
        keep_start = [
            jnp.where((reset >= g0) & (reset <= g0 + f), 0.0, 1.0).astype(F32)
            for f in range(TILE_FRAMES)
        ]
        decay = wide_decays(steps_ref[...].reshape(half, heads), heads, width)
        before = [frame_rows(decay, 0)]
        for f in range(1, TILE_FRAMES):
            before.append(before[-1] * frame_rows(decay, f))
        after = [jnp.ones((OCTET, width), F32)]
        for f in range(TILE_FRAMES - 1, 0, -1):
            after.append(after[-1] * frame_rows(decay, f))
        after = jnp.concatenate(after[::-1], axis=0)
        back = 1.0 / before[-1]
        relative = jnp.concatenate([b * back for b in before], axis=0)
        from_base = jnp.concatenate([b * s for b, s in zip(before, keep_start)], axis=0)
        inner = mixed_ref[:, width : 2 * width].astype(F32)
        ww, rr = twice_each(mixed_ref[:, 2 * width :].astype(F32), state)
        rr_ref[...] = rr.astype(BF16)
        gram = nt_dot(rr.astype(BF16), ww.astype(BF16)) * 0.5
        gram = jnp.where(joined, gram, 0.0).astype(BF16)
        near = nn_dot(gram, (inner * after).astype(BF16)) * relative
        far = nn_dot(spread_read(rr, state), entry_ref[0]) * from_base
        gate = mixed_ref[:, :width].astype(F32)
        silu = gate / (1.0 + jnp.exp(-gate))
        z_ref[...] = ((near + far) * mixer_scale + skip_row * inner) * silu
        start = reach_ref[0] * mixer_scale
        reached = jnp.concatenate(
            [start * frame_rows(from_base, f) for f in range(TILE_FRAMES)], axis=0
        )
        ag_ref[...] = (reached * silu).astype(BF16)

    total = tiles * half

    def row_block(cols):
        return pl.BlockSpec((half, cols), lambda i: (i, 0))

    return pl.pallas_call(
        body,
        grid=(tiles,),
        in_specs=[
            whole(ids.shape),
            SMEM_SPEC,
            pl.BlockSpec((TILE_FRAMES, OCTET, heads), lambda i: (c * tiles + i, o, 0)),
            pl.BlockSpec((half, mixed.shape[1]), lambda i: (i * octet_count + o, 0)),
            pl.BlockSpec((1, octet_state, width), lambda i: (i, o, 0)),
            pl.BlockSpec((1, OCTET, width), lambda i: (i, o, 0)),
        ],
        out_specs=[row_block(width), row_block(width), row_block(LANES)],
        out_shape=[
            jax.ShapeDtypeStruct((total, width), F32),
            jax.ShapeDtypeStruct((total, width), BF16),
            jax.ShapeDtypeStruct((total, LANES), BF16),
        ],
        compiler_params=grant(14),
        name="scan",
    )(ids, skip, steps, mixed, entry, reach)


def decay_rows(tail, n):
    tail = tail.astype(F32)
    return [tail[8 * i : 8 * i + 1] + tail[8 * i + 4 : 8 * i + 5] for i in range(n)]


def residues_of(pay, state):
    return pay // (state + 8)


def group_total(got, after, state):
    pay, width = got[0].shape
    n = residues_of(pay, state)
    body_rows = n * state

    def body(*refs):
        got_refs = refs[:GROUP]
        out_ref, sorted_s = refs[-2:]
        place = my_place()
        for k in range(GROUP):
            sorted_s[place ^ k] = got_refs[k][...]
        tails = [decay_rows(sorted_s[j, body_rows:], n) for j in range(GROUP)]
        sub = lax.broadcasted_iota(jnp.int32, (CARRY_ROWS, width), 0) % 8
        lines = []
        for i in range(n):
            rs = slice(i * state, (i + 1) * state)
            total = sorted_s[0, rs].astype(F32)
            product = tails[0][i]
            for j in range(1, GROUP):
                total = total * tails[j][i] + sorted_s[j, rs].astype(F32)
                product = product * tails[j][i]
            out_ref[rs] = total.astype(BF16)
            lines.append(jnp.broadcast_to(product, (8, width)))
        for i in range(0, n, 2):
            value = jnp.concatenate(lines[i : i + 2], axis=0)
            upper = value.astype(BF16).astype(F32)
            lo = body_rows + 8 * i
            out_ref[lo : lo + 16] = jnp.where(sub < 4, upper, value - upper).astype(BF16)

    return pl.pallas_call(
        body,
        grid=(1,),
        in_specs=[whole((pay, width))] * GROUP + [HBM_SPEC] * len(after),
        out_specs=whole((pay, width)),
        out_shape=jax.ShapeDtypeStruct((pay, width), BF16),
        scratch_shapes=[pltpu.VMEM((GROUP, pay, width), BF16)],
        compiler_params=grant(6),
        name="group_total",
    )(*got, *after)


def group_prefixes(got, entering, after, state):
    pay, width = got[0].shape
    n = residues_of(pay, state)
    body_rows = n * state

    def body(*refs):
        got_refs, in_ref = refs[:GROUP], refs[GROUP]
        out_refs = refs[-GROUP - 2 : -2]
        sorted_s, prefix_s = refs[-2:]
        place = my_place()
        for k in range(GROUP):
            sorted_s[place ^ k] = got_refs[k][...]
        tails = [decay_rows(sorted_s[j, body_rows:], n) for j in range(GROUP)]
        for i in range(n):
            rs = slice(i * state, (i + 1) * state)
            total = in_ref[rs].astype(F32)
            prefix_s[0, rs] = total.astype(BF16)
            for j in range(GROUP - 1):
                total = total * tails[j][i] + sorted_s[j, rs].astype(F32)
                prefix_s[j + 1, rs] = total.astype(BF16)
        for k in range(GROUP):
            out_refs[k][...] = prefix_s[place ^ k]

    spec = whole((pay, width))
    out = whole((body_rows, width))
    return pl.pallas_call(
        body,
        grid=(1,),
        in_specs=[spec] * (GROUP + 1) + [HBM_SPEC] * len(after),
        out_specs=[out] * GROUP,
        out_shape=[jax.ShapeDtypeStruct((body_rows, width), BF16)] * GROUP,
        scratch_shapes=[
            pltpu.VMEM((GROUP, pay, width), BF16),
            pltpu.VMEM((GROUP, body_rows, width), BF16),
        ],
        compiler_params=grant(8),
        name="group_prefixes",
    )(*got, entering, *after)


def join_payloads(earlier, later, state):
    n = residues_of(later.shape[0], state)
    body_rows = n * state
    width = later.shape[1]
    early = decay_rows(earlier[body_rows:], n)
    late = decay_rows(later[body_rows:], n)
    parts, lines = [], []
    for i in range(n):
        rs = slice(i * state, (i + 1) * state)
        parts.append(earlier[rs].astype(F32) * late[i] + later[rs].astype(F32))
        value = early[i] * late[i]
        upper = value.astype(BF16).astype(F32)
        lines += [jnp.broadcast_to(upper, (4, width)), jnp.broadcast_to(value - upper, (4, width))]
    return jnp.concatenate(parts + lines, axis=0).astype(BF16)


def states_entering(payloads, covers, state, tm_size):
    groups = tm_size // GROUP
    order = list(range(GROUP - 1, 0, -1))

    def swap(parts):
        moved = {
            k: lax.ppermute(parts[k], "tm", [(i, i ^ k) for i in range(tm_size)]) for k in order
        }
        return [parts[0]] + [moved[k] for k in range(1, GROUP)]

    def onward(value, hops):
        moved = hops * GROUP
        return lax.ppermute(value, "tm", [(i, i + moved) for i in range(tm_size - moved)])

    octet_count = len(payloads) // GROUP
    gathered = [swap(payloads[e * GROUP : (e + 1) * GROUP]) for e in range(octet_count)]
    result = []
    for e, got in enumerate(gathered):
        total = group_total(got, [] if e else covers[:1], state)
        entering = onward(total, 1) if groups > 1 else jnp.zeros_like(total)
        hops = 1
        while hops < groups - 1:
            entering = join_payloads(onward(entering, hops), entering, state)
            hops *= 2
        result.append(swap(group_prefixes(got, entering, [] if e else covers[1:], state)))
    return result


def finish_octet(o, c, entered, mid, z, ag, rr, w_mix, frames, res, state, ready, done, after):
    total, width = mid.shape
    octet_count = res // OCTET
    half = TILE_FRAMES * OCTET
    tiles = total // (half * octet_count)
    piece = entered[0].shape[0]
    last = o == octet_count - 1
    done_args = [] if done is None else [done]

    def body(*refs):
        in_refs = refs[:GROUP]
        mid_ref, z_ref, ag_ref, rr_ref, w_ref = refs[GROUP : GROUP + 5]
        ready_refs = refs[GROUP + 5 : GROUP + 5 + len(ready)]
        out_ref, state_s = refs[-2:]

        @pl.when(pl.program_id(0) == 0)
        def _():
            place = my_place()
            for k in range(GROUP):
                state_s[place ^ k] = in_refs[k][...]

        read = spread_read(rr_ref[...].astype(F32), state)
        far = nn_dot(read, state_s[...].reshape(GROUP * piece, width))
        gated = (z_ref[...] + ag_ref[...].astype(F32) * far).astype(BF16)
        out = mid_ref[...] + nn_dot(gated, w_ref[...])
        if not last:
            out_ref[...] = out.astype(BF16)
            return
        cubes = [r[...].astype(F32) for r in ready_refs] + [out]
        cubes = [x.reshape(TILE_FRAMES, OCTET, width) for x in cubes]
        out_ref[...] = jnp.concatenate(cubes, axis=1).astype(BF16)

    def rows_of(cols):
        return pl.BlockSpec((half, cols), lambda i: (i, 0))

    octet_rows = rows_of(width)
    if last:
        out_spec = pl.BlockSpec((TILE_FRAMES, res, width), lambda i: (c * tiles + i, 0, 0))
        out_shape = jax.ShapeDtypeStruct((frames, res, width), BF16)
    else:
        out_spec = octet_rows
        out_shape = jax.ShapeDtypeStruct((tiles * half, width), BF16)
    n_in = GROUP + 5 + len(ready)
    return pl.pallas_call(
        body,
        grid=(tiles,),
        in_specs=[whole((piece, width))] * GROUP
        + [pl.BlockSpec((half, width), lambda i: (i * octet_count + o, 0))]
        + [rows_of(width), rows_of(width), rows_of(LANES)]
        + [whole(w_mix.shape)]
        + [octet_rows] * len(ready)
        + [HBM_SPEC] * (len(done_args) + len(after)),
        out_specs=out_spec,
        out_shape=out_shape,
        scratch_shapes=[pltpu.VMEM((GROUP, piece, width), BF16)],
        input_output_aliases={n_in: 0} if done_args else {},
        compiler_params=grant(14),
        name="finish",
    )(*entered, mid, z, ag, rr, w_mix, *ready, *done_args, *after)


def local(
    tokens,
    cond_mask,
    cond_embed,
    attn_gain,
    w_qkv,
    w_out,
    mix_gain,
    w_in,
    decay_steps,
    segment_ids,
    skip_gain,
    w_mix_out,
):
    frames, res, width = tokens.shape
    heads = skip_gain.shape[0]
    state = (w_in.shape[1] - 2 * width) // 2
    tm_size = lax.axis_size("tm")
    peers = lax.axis_size("res")
    part = PART_FRAMES
    chunks = frames // (part * peers)
    order = list(range(peers - 1, 0, -1))

    def swap(value, k):
        return lax.ppermute(value, "res", [(i, i ^ k) for i in range(peers)])

    ids = segment_ids.reshape(-1, LANES)
    pieces = prepare(tokens, [], chunks, peers)
    gathered = []
    for c in range(chunks):
        mine = pieces[c * peers : (c + 1) * peers]
        got = {k: swap(mine[k], k) for k in order}
        got[0] = mine[0]
        gathered.append([got[k] for k in range(peers)])

    embed = cond_embed.reshape(-1, LANES)
    first_gain = attn_gain.reshape(-1, LANES)
    second_gain = mix_gain.reshape(-1, LANES)
    mixer_scale = 1.0 / math.sqrt(frames * tm_size * state)

    attended = []
    for c in range(chunks):
        outs = attend_chunk(
            cond_mask,
            gathered[c],
            embed,
            first_gain,
            w_qkv,
            c * part * peers,
            heads,
            [] if c else [decay_steps],
        )
        back = {k: swap(outs[k], k) for k in order}
        back[0] = outs[0]
        attended.append([back[k] for k in range(peers)])

    octet_count = res // OCTET

    def scan(o, c):
        _, mixed, entry, reach = held[c]
        return scan_octet(
            o, c, frames, ids, skip_gain, decay_steps, mixed, entry, reach, mixer_scale
        )

    carry, held, scanned = None, [], []
    for c in range(chunks):
        after = [rr for _, _, rr in scanned[-1]] if scanned else []
        out, carry = mix_chunk(
            c,
            chunks,
            cond_mask,
            ids,
            tokens,
            attended[c],
            decay_steps,
            embed,
            second_gain,
            w_out,
            w_in,
            carry,
            after,
        )
        held.append(out)
        scanned.append([scan(o, c) for o in range(octet_count)])
    covers = [rr for _, _, rr in scanned[-1]]
    entered = states_entering(carry, covers[:1], state, tm_size)
    ready = [[] for _ in range(chunks)]
    done = None
    for o in range(octet_count):
        for c in range(chunks):
            z, ag, rr = scanned[c][o]
            out = finish_octet(
                o,
                c,
                entered[o],
                held[c][0],
                z,
                ag,
                rr,
                w_mix_out,
                frames,
                res,
                state,
                ready[c],
                done,
                [] if o else covers[1:],
            )
            if o < octet_count - 1:
                ready[c] = ready[c] + [out]
            else:
                done, ready[c] = out, []
    return done


def solution(mesh):
    in_specs = (
        P("tm", "res", None),
        P("tm"),
        P(),
        P(),
        P(),
        P(),
        P(),
        P(),
        P("tm", "res", None),
        P(),
        P(),
        P(),
    )
    out_specs = P("tm", "res", None)
    return jax.shard_map(local, mesh=mesh, in_specs=in_specs, out_specs=out_specs, check_vma=False)
```

```python
import math

import jax
import jax.numpy as jnp
from jax import lax
from jax.experimental import pallas as pl
from jax.experimental.pallas import tpu as pltpu
from jax.sharding import PartitionSpec as P


BF16 = jnp.bfloat16
F32 = jnp.float32
LANES = 128
PART_FRAMES = 16
STAGE_FRAMES = 4
TILE_FRAMES = 32
OCTET = 8
GROUP = 4
CARRY_ROWS = 16


def rms_rows(rows, gain):
    mean = jnp.mean(rows * rows, axis=-1, keepdims=True)
    return rows * lax.rsqrt(mean + 1e-06) * gain


def nt_dot(a, b):
    return lax.dot_general(a, b, (((1,), (1,)), ((), ())), preferred_element_type=F32)


def tn_dot(a, b):
    return lax.dot_general(a, b, (((0,), (0,)), ((), ())), preferred_element_type=F32)


def nn_dot(a, b):
    return jnp.dot(a, b, preferred_element_type=F32)


def joined_row(ref):
    return jnp.concatenate([ref[i : i + 1] for i in range(ref.shape[0])], axis=1)


def first_reset(ids_ref, frames):
    ids = ids_ref[...]
    first = (ids == jnp.min(ids)).astype(F32)
    return jnp.sum(first).astype(jnp.int32) - lax.axis_index("tm") * frames


def my_place():
    return lax.axis_index("tm") % GROUP


def whole(shape):
    return pl.BlockSpec(shape, lambda i: (0,) * len(shape))


def grant(mib):
    return pltpu.CompilerParams(vmem_limit_bytes=mib << 20)


SMEM_SPEC = pl.BlockSpec(memory_space=pltpu.SMEM)
HBM_SPEC = pl.BlockSpec(memory_space=pl.ANY)


def prepare(tokens, after, chunks, peers):
    frames, res, width = tokens.shape
    part = frames // (chunks * peers)
    count = chunks * peers

    def body(*refs):
        tok_ref, out_refs = refs[0], refs[-count:]
        me = lax.axis_index("res")
        for c in range(chunks):
            for k in range(peers):
                start = c * part * peers + (me ^ k) * part
                out_refs[c * peers + k][...] = tok_ref[pl.ds(start, part)]

    piece = (part, res, width)
    return pl.pallas_call(
        body,
        grid=(1,),
        in_specs=[whole(tokens.shape)] + [HBM_SPEC] * len(after),
        out_specs=[whole(piece)] * count,
        out_shape=[jax.ShapeDtypeStruct(piece, tokens.dtype)] * count,
        compiler_params=grant(10),
        name="prepare",
    )(tokens, *after)


def attend_chunk(cond, parts, embed, gain, w_qkv, first_frame, heads, follow):
    peers = len(parts)
    frames, res, width = parts[0].shape
    head_size = width // heads
    keys = peers * res
    pairs = width // LANES
    inv_root = 1.0 / math.sqrt(head_size)

    def body(cond_ref, *refs):
        tok_refs = refs[:peers]
        embed_ref, gain_ref, w_ref = refs[peers : peers + 3]
        out_refs = refs[-peers - 2 : -2]
        norm_s, qkv_s = refs[-2:]
        me = lax.axis_index("res")
        embed_row = joined_row(embed_ref)
        gain_row = joined_row(gain_ref)
        for f in range(frames):
            flag = cond_ref[first_frame + me * frames + f].astype(F32)
            added = flag * embed_row
            for k in range(peers):
                rows = tok_refs[k][f].astype(F32) + added
                norm_s[k, f] = rms_rows(rows, gain_row).astype(BF16)
        flat = norm_s[...].reshape(peers * frames * res, width)
        shape = (peers, frames, res)
        got = nn_dot(flat, w_ref[:, : 2 * width]).astype(BF16)
        scaled = got[:, :width] * jnp.asarray(inv_root, BF16)
        qkv_s[:, :, :, :width] = scaled.reshape(*shape, width)
        qkv_s[:, :, :, width : 2 * width] = got[:, width:].reshape(*shape, width)
        got = nn_dot(flat, w_ref[:, 2 * width :]).astype(BF16)
        qkv_s[:, :, :, 2 * width :] = got.reshape(*shape, width)
        lane = lax.broadcasted_iota(jnp.int32, (1, LANES), 1)
        first = (lane < head_size).astype(BF16)
        second = (lane >= head_size).astype(BF16)
        pick = lax.broadcasted_iota(jnp.int32, (keys, LANES), 1) < head_size

        def stage(f0):
            units = [(f0 + f, p) for f in range(STAGE_FRAMES) for p in range(pairs)]

            def part(n, f, p):
                lo = n * width + p * LANES
                return qkv_s[:, pl.ds(f, 1), :, lo : lo + LANES].reshape(keys, LANES)

            scores = []
            for f, p in units:
                q = part(0, f, p)
                stacked = jnp.concatenate([q * first, q * second], axis=0)
                scores.append(nt_dot(part(1, f, p), stacked))
            tops = [jnp.max(x, axis=0, keepdims=True) for x in scores]
            weights = [jnp.exp(x - t) for x, t in zip(scores, tops)]
            totals = [jnp.sum(w, axis=0, keepdims=True) for w in weights]
            weights = [(w * (1.0 / t)).astype(BF16) for w, t in zip(weights, totals)]
            both = [tn_dot(w, part(2, f, p)) for w, (f, p) in zip(weights, units)]
            for got, (f, p) in zip(both, units):
                att = jnp.where(pick, got[:keys], got[keys:]).astype(BF16)
                for k in range(peers):
                    out_refs[k][pl.ds(f, 1), :, p * LANES : (p + 1) * LANES] = att[
                        k * res : (k + 1) * res
                    ].reshape(1, res, LANES)

        def step(i, _):
            stage(i * STAGE_FRAMES)
            return 0

        lax.fori_loop(0, frames // STAGE_FRAMES, step, 0)

    block = whole((frames, res, width))
    return pl.pallas_call(
        body,
        grid=(1,),
        in_specs=[SMEM_SPEC]
        + [block] * peers
        + [whole(a.shape) for a in (embed, gain, w_qkv)]
        + [HBM_SPEC] * len(follow),
        out_specs=[block] * peers,
        out_shape=[jax.ShapeDtypeStruct((frames, res, width), BF16)] * peers,
        scratch_shapes=[
            pltpu.VMEM((peers, frames, res, width), BF16),
            pltpu.VMEM((peers, frames, res, 3 * width), BF16),
        ],
        compiler_params=grant(14),
        name="attend",
    )(cond, *parts, embed, gain, w_qkv, *follow)


def octets(rows, frames, res):
    n = rows.shape[-1]
    cube = rows.reshape(frames, res, n)
    return [
        cube[:, o * OCTET : (o + 1) * OCTET].reshape(frames * OCTET, n) for o in range(res // OCTET)
    ]


def wide_decays(steps, heads, width):
    values = 1.0 - steps.astype(F32) * (1.0 / 4096.0)
    rows = values.shape[0]
    head_size = width // heads
    per = LANES // head_size
    lane_head = lax.broadcasted_iota(jnp.int32, (rows, LANES), 1) // head_size
    parts = []
    for p in range(width // LANES):
        part = jnp.broadcast_to(values[:, p * per : p * per + 1], (rows, LANES))
        for h in range(1, per):
            col = values[:, p * per + h : p * per + h + 1]
            part = jnp.where(lane_head == h, jnp.broadcast_to(col, (rows, LANES)), part)
        parts.append(part)
    return jnp.concatenate(parts, axis=1)


def frame_rows(value, f):
    return value[f * OCTET : (f + 1) * OCTET]


def twice_each(maps, state):
    low = lax.broadcasted_iota(jnp.int32, maps.shape, 1) < state
    turned = pltpu.roll(maps, state, 1)
    return jnp.where(low, maps, turned), jnp.where(low, turned, maps)


def spread_read(rr, state):
    rows = rr.shape[0]
    mine = lax.broadcasted_iota(jnp.int32, (rows, LANES), 0) % OCTET
    lane = lax.broadcasted_iota(jnp.int32, (rows, LANES), 1) // state
    per = LANES // state
    return jnp.concatenate(
        [jnp.where(mine - j * per == lane, rr, 0.0).astype(BF16) for j in range(OCTET // per)],
        axis=1,
    )


def mix_chunk(c, chunks, cond, ids, tokens, attended, steps, embed, gain, w_out, w_in, carry, follow):
    frames_all, res, width = tokens.shape
    heads = steps.shape[-1]
    peers = len(attended)
    part_frames = attended[0].shape[0]
    frames = part_frames * peers
    tiles = frames // TILE_FRAMES
    rows = TILE_FRAMES * res
    half = TILE_FRAMES * OCTET
    mixed_width = w_in.shape[1]
    state = (mixed_width - 2 * width) // 2
    spread = res * state
    last = c == chunks - 1
    pays = GROUP * (res // OCTET)
    per_pay = OCTET // GROUP
    pay_rows = per_pay * state
    carry_args = [] if carry is None else list(carry)
    n_in = 8 + peers

    def body(*refs):
        cond_ref, ids_ref, tok_ref = refs[:3]
        att_refs = refs[3 : 3 + peers]
        steps_ref, embed_ref, gain_ref, wo_ref, wi_ref = refs[3 + peers : n_in]
        pos = n_in + len(carry_args)
        carry_refs = refs[n_in:pos]
        pos += len(follow)
        mid_ref, mixed_ref, entry_ref, reach_ref = refs[pos : pos + 4]
        pos += 4
        pay_refs = refs[pos : pos + pays] if last else ()
        pos += len(pay_refs)
        if last:
            att_s, s_ref, p_ref, p_wide = refs[pos:]
        else:
            s_ref, p_ref, att_s = refs[pos:]
        reset = first_reset(ids_ref, frames_all)
        me, place = lax.axis_index("res"), my_place()
        for k in range(peers):
            att_s[me ^ k] = att_refs[k][...]
        if carry is None:
            s_ref[...] = jnp.zeros_like(s_ref)
            p_ref[...] = jnp.ones_like(p_ref)
        else:
            s_ref[...] = carry_refs[0][...]
            p_ref[...] = carry_refs[1][...]
        embed_row = joined_row(embed_ref)
        gain_row = joined_row(gain_ref)
        att_all = att_s[...].reshape(frames * res, width)
        for i in range(tiles):
            g0 = c * frames + i * TILE_FRAMES
            g_end = g0 + TILE_FRAMES - 1
            sl = slice(i * rows, (i + 1) * rows)
            hidden = jnp.concatenate(
                [
                    tok_ref[i * TILE_FRAMES + f].astype(F32)
                    + cond_ref[g0 + f].astype(F32) * embed_row
                    for f in range(TILE_FRAMES)
                ],
                axis=0,
            )
            mid = hidden + nn_dot(att_all[sl], wo_ref[...])
            mid_ref[sl] = jnp.concatenate(octets(mid, TILE_FRAMES, res), axis=0)
            mixer_in = rms_rows(mid, gain_row)
            mixer_in = jnp.concatenate(octets(mixer_in, TILE_FRAMES, res), axis=0).astype(BF16)
            mixed_ref[sl, width:] = nn_dot(mixer_in, wi_ref[:, width:]).astype(BF16)
            mixed_ref[sl, :width] = mixer_in
            tile_steps = steps_ref[i * TILE_FRAMES : (i + 1) * TILE_FRAMES]
            keep_end = [
                jnp.where((reset > g0 + f) & (reset <= g_end), 0.0, 1.0).astype(F32)
                for f in range(TILE_FRAMES)
            ]
            keep_all = jnp.where((reset >= g0) & (reset <= g_end), 0.0, 1.0).astype(F32)
            entry_ref[i] = s_ref[...].astype(BF16)
            reach_ref[i] = p_ref[...]
            for o in range(res // OCTET):
                os = slice(i * rows + o * half, i * rows + (o + 1) * half)
                st = tile_steps[:, o * OCTET : (o + 1) * OCTET].reshape(half, heads)
                decay = wide_decays(st, heads, width)
                after = [jnp.ones((OCTET, width), F32)]
                for f in range(TILE_FRAMES - 1, 0, -1):
                    after.append(after[-1] * frame_rows(decay, f))
                transit = after[-1] * frame_rows(decay, 0) * keep_all
                after = after[::-1]
                kept = jnp.concatenate([a * s for a, s in zip(after, keep_end)], axis=0)
                inner = mixed_ref[os, width : 2 * width].astype(F32)
                kept = (inner * kept).astype(BF16)
                maps = mixed_ref[os, 2 * width :].astype(F32)
                write_t = maps.T[:state]
                col = lax.broadcasted_iota(jnp.int32, (state, half), 1) % OCTET
                write = jnp.concatenate(
                    [jnp.where(col == r, write_t, 0.0).astype(BF16) for r in range(OCTET)], axis=0
                )
                added = nn_dot(write, kept)
                for r in range(OCTET):
                    rs = slice(r * state, (r + 1) * state)
                    ss = slice((o * OCTET + r) * state, (o * OCTET + r + 1) * state)
                    s_ref[ss] = s_ref[ss] * transit[r : r + 1] + added[rs]
                po = slice(o * OCTET, (o + 1) * OCTET)
                p_ref[po] = p_ref[po] * transit
        if not last:
            return
        p_all = p_ref[...]
        for r in range(res):
            p_wide[r] = jnp.broadcast_to(p_all[r : r + 1], (8, width))
        sub = lax.broadcasted_iota(jnp.int32, (CARRY_ROWS, width), 0) % 8
        for e in range(res // OCTET):
            for k in range(GROUP):
                r0 = e * OCTET + (place ^ k) * per_pay
                out = pay_refs[e * GROUP + k]
                start = pl.multiple_of(r0 * state, pay_rows)
                out[:pay_rows] = s_ref[pl.ds(start, pay_rows), :].astype(BF16)
                for n in range(0, per_pay, 2):
                    value = jnp.concatenate([p_wide[r0 + n], p_wide[r0 + n + 1]], axis=0)
                    upper = value.astype(BF16).astype(F32)
                    lo = pay_rows + n * 8
                    out[lo : lo + 16] = jnp.where(sub < 4, upper, value - upper).astype(BF16)

    chunk_rows = frames * res
    in_specs = (
        [SMEM_SPEC, whole(ids.shape)]
        + [pl.BlockSpec((frames, res, width), lambda i: (c, 0, 0))]
        + [whole(attended[0].shape)] * peers
        + [pl.BlockSpec((frames, res, heads), lambda i: (c, 0, 0))]
        + [whole(a.shape) for a in (embed, gain, w_out, w_in)]
        + [whole(a.shape) for a in carry_args]
        + [HBM_SPEC] * len(follow)
    )
    out_shape = [
        jax.ShapeDtypeStruct((chunk_rows, width), F32),
        jax.ShapeDtypeStruct((chunk_rows, mixed_width), BF16),
        jax.ShapeDtypeStruct((tiles, spread, width), BF16),
        jax.ShapeDtypeStruct((tiles, res, width), F32),
    ]
    scratch = [pltpu.VMEM((peers, part_frames, res, width), BF16)]
    if last:
        pay = (pay_rows + 8 * per_pay, width)
        out_shape += [jax.ShapeDtypeStruct(pay, BF16)] * pays
        scratch += [
            pltpu.VMEM((spread, width), F32),
            pltpu.VMEM((res, width), F32),
            pltpu.VMEM((res, 8, width), F32),
        ]
    else:
        out_shape += [
            jax.ShapeDtypeStruct((spread, width), F32),
            jax.ShapeDtypeStruct((res, width), F32),
        ]
    outs = pl.pallas_call(
        body,
        grid=(1,),
        in_specs=in_specs,
        out_specs=[whole(o.shape) for o in out_shape],
        out_shape=out_shape,
        scratch_shapes=scratch,
        compiler_params=grant(20),
        name="mix",
    )(cond, ids, tokens, *attended, steps, embed, gain, w_out, w_in, *carry_args, *follow)
    return outs[:4], outs[4:]


def scan_octet(o, c, frames_all, ids, skip, steps, mixed, entry, reach, w_in, mixer_scale):
    tiles, spread, width = entry.shape
    _, res, heads = steps.shape
    state = spread // res
    half = TILE_FRAMES * OCTET
    octet_state = OCTET * state
    octet_count = res // OCTET

    def body(
        ids_ref,
        skip_ref,
        steps_ref,
        mixed_ref,
        entry_ref,
        reach_ref,
        wg_ref,
        z_ref,
        ag_ref,
        rr_ref,
    ):
        reset = first_reset(ids_ref, frames_all)
        feature = lax.broadcasted_iota(jnp.int32, (1, width), 1) // (width // heads)
        skip_row = jnp.zeros((1, width), F32)
        for h in range(heads):
            skip_row = jnp.where(feature == h, skip_ref[h], skip_row)
        g0 = c * tiles * TILE_FRAMES + pl.program_id(0) * TILE_FRAMES
        row_i = lax.broadcasted_iota(jnp.int32, (half, half), 0)
        col_i = lax.broadcasted_iota(jnp.int32, (half, half), 1)
        edge = (reset - g0) * OCTET
        joined = (
            ((row_i % OCTET) == (col_i % OCTET))
            & (row_i >= col_i)
            & ((row_i >= edge) == (col_i >= edge))
        )
        keep_start = [
            jnp.where((reset >= g0) & (reset <= g0 + f), 0.0, 1.0).astype(F32)
            for f in range(TILE_FRAMES)
        ]
        decay = wide_decays(steps_ref[...].reshape(half, heads), heads, width)
        before = [frame_rows(decay, 0)]
        for f in range(1, TILE_FRAMES):
            before.append(before[-1] * frame_rows(decay, f))
        after = [jnp.ones((OCTET, width), F32)]
        for f in range(TILE_FRAMES - 1, 0, -1):
            after.append(after[-1] * frame_rows(decay, f))
        after = jnp.concatenate(after[::-1], axis=0)
        back = 1.0 / before[-1]
        relative = jnp.concatenate([b * back for b in before], axis=0)
        from_base = jnp.concatenate([b * s for b, s in zip(before, keep_start)], axis=0)
        inner = mixed_ref[:, width : 2 * width].astype(F32)
        ww, rr = twice_each(mixed_ref[:, 2 * width :].astype(F32), state)
        rr_ref[...] = rr.astype(BF16)
        gram = nt_dot(rr.astype(BF16), ww.astype(BF16)) * 0.5
        gram = jnp.where(joined, gram, 0.0).astype(BF16)
        near = nn_dot(gram, (inner * after).astype(BF16)) * relative
        far = nn_dot(spread_read(rr, state), entry_ref[0]) * from_base
        gate = nn_dot(mixed_ref[:, :width], wg_ref[...]).astype(BF16).astype(F32)
        gate = 0.5 * gate
        silu = gate + gate * jnp.tanh(gate)
        z_ref[...] = ((near + far) * mixer_scale + skip_row * inner) * silu
        start = reach_ref[0] * mixer_scale
        reached = jnp.concatenate(
            [start * frame_rows(from_base, f) for f in range(TILE_FRAMES)], axis=0
        )
        ag_ref[...] = (reached * silu).astype(BF16)

    total = tiles * half

    def row_block(cols):
        return pl.BlockSpec((half, cols), lambda i: (i, 0))

    return pl.pallas_call(
        body,
        grid=(tiles,),
        in_specs=[
            whole(ids.shape),
            SMEM_SPEC,
            pl.BlockSpec((TILE_FRAMES, OCTET, heads), lambda i: (c * tiles + i, o, 0)),
            pl.BlockSpec((half, mixed.shape[1]), lambda i: (i * octet_count + o, 0)),
            pl.BlockSpec((1, octet_state, width), lambda i: (i, o, 0)),
            pl.BlockSpec((1, OCTET, width), lambda i: (i, o, 0)),
            whole((width, width)),
        ],
        out_specs=[row_block(width), row_block(width), row_block(LANES)],
        out_shape=[
            jax.ShapeDtypeStruct((total, width), F32),
            jax.ShapeDtypeStruct((total, width), BF16),
            jax.ShapeDtypeStruct((total, LANES), BF16),
        ],
        compiler_params=grant(14),
        name="scan",
    )(ids, skip, steps, mixed, entry, reach, w_in)


def decay_rows(tail, n):
    tail = tail.astype(F32)
    return [tail[8 * i : 8 * i + 1] + tail[8 * i + 4 : 8 * i + 5] for i in range(n)]


def residues_of(pay, state):
    return pay // (state + 8)


def group_total(got, after, state):
    pay, width = got[0].shape
    n = residues_of(pay, state)
    body_rows = n * state

    def body(*refs):
        got_refs = refs[:GROUP]
        out_ref, sorted_s = refs[-2:]
        place = my_place()
        for k in range(GROUP):
            sorted_s[place ^ k] = got_refs[k][...]
        tails = [decay_rows(sorted_s[j, body_rows:], n) for j in range(GROUP)]
        sub = lax.broadcasted_iota(jnp.int32, (CARRY_ROWS, width), 0) % 8
        lines = []
        for i in range(n):
            rs = slice(i * state, (i + 1) * state)
            total = sorted_s[0, rs].astype(F32)
            product = tails[0][i]
            for j in range(1, GROUP):
                total = total * tails[j][i] + sorted_s[j, rs].astype(F32)
                product = product * tails[j][i]
            out_ref[rs] = total.astype(BF16)
            lines.append(jnp.broadcast_to(product, (8, width)))
        for i in range(0, n, 2):
            value = jnp.concatenate(lines[i : i + 2], axis=0)
            upper = value.astype(BF16).astype(F32)
            lo = body_rows + 8 * i
            out_ref[lo : lo + 16] = jnp.where(sub < 4, upper, value - upper).astype(BF16)

    return pl.pallas_call(
        body,
        grid=(1,),
        in_specs=[whole((pay, width))] * GROUP + [HBM_SPEC] * len(after),
        out_specs=whole((pay, width)),
        out_shape=jax.ShapeDtypeStruct((pay, width), BF16),
        scratch_shapes=[pltpu.VMEM((GROUP, pay, width), BF16)],
        compiler_params=grant(6),
        name="group_total",
    )(*got, *after)


def group_prefixes(got, entering, after, state):
    pay, width = got[0].shape
    n = residues_of(pay, state)
    body_rows = n * state

    def body(*refs):
        got_refs, in_ref = refs[:GROUP], refs[GROUP]
        out_refs = refs[-GROUP - 2 : -2]
        sorted_s, prefix_s = refs[-2:]
        place = my_place()
        for k in range(GROUP):
            sorted_s[place ^ k] = got_refs[k][...]
        tails = [decay_rows(sorted_s[j, body_rows:], n) for j in range(GROUP)]
        for i in range(n):
            rs = slice(i * state, (i + 1) * state)
            total = in_ref[rs].astype(F32)
            prefix_s[0, rs] = total.astype(BF16)
            for j in range(GROUP - 1):
                total = total * tails[j][i] + sorted_s[j, rs].astype(F32)
                prefix_s[j + 1, rs] = total.astype(BF16)
        for k in range(GROUP):
            out_refs[k][...] = prefix_s[place ^ k]

    spec = whole((pay, width))
    out = whole((body_rows, width))
    return pl.pallas_call(
        body,
        grid=(1,),
        in_specs=[spec] * (GROUP + 1) + [HBM_SPEC] * len(after),
        out_specs=[out] * GROUP,
        out_shape=[jax.ShapeDtypeStruct((body_rows, width), BF16)] * GROUP,
        scratch_shapes=[
            pltpu.VMEM((GROUP, pay, width), BF16),
            pltpu.VMEM((GROUP, body_rows, width), BF16),
        ],
        compiler_params=grant(8),
        name="group_prefixes",
    )(*got, entering, *after)


def join_payloads(earlier, later, state):
    n = residues_of(later.shape[0], state)
    body_rows = n * state
    width = later.shape[1]
    early = decay_rows(earlier[body_rows:], n)
    late = decay_rows(later[body_rows:], n)
    parts, lines = [], []
    for i in range(n):
        rs = slice(i * state, (i + 1) * state)
        parts.append(earlier[rs].astype(F32) * late[i] + later[rs].astype(F32))
        value = early[i] * late[i]
        upper = value.astype(BF16).astype(F32)
        lines += [jnp.broadcast_to(upper, (4, width)), jnp.broadcast_to(value - upper, (4, width))]
    return jnp.concatenate(parts + lines, axis=0).astype(BF16)


def states_entering(payloads, covers, state, tm_size):
    groups = tm_size // GROUP
    order = list(range(GROUP - 1, 0, -1))

    def swap(parts):
        moved = {
            k: lax.ppermute(parts[k], "tm", [(i, i ^ k) for i in range(tm_size)]) for k in order
        }
        return [parts[0]] + [moved[k] for k in range(1, GROUP)]

    def onward(value, hops):
        moved = hops * GROUP
        return lax.ppermute(value, "tm", [(i, i + moved) for i in range(tm_size - moved)])

    octet_count = len(payloads) // GROUP
    gathered = [swap(payloads[e * GROUP : (e + 1) * GROUP]) for e in range(octet_count)]
    result = []
    for e, got in enumerate(gathered):
        total = group_total(got, [] if e else covers[:1], state)
        entering = onward(total, 1) if groups > 1 else jnp.zeros_like(total)
        hops = 1
        while hops < groups - 1:
            entering = join_payloads(onward(entering, hops), entering, state)
            hops *= 2
        result.append(swap(group_prefixes(got, entering, [] if e else covers[1:], state)))
    return result


def finish_octet(o, entered, mids, scanned, w_mix, frames, res, state, ready):
    total, width = mids[0].shape
    octet_count = res // OCTET
    half = TILE_FRAMES * OCTET
    chunks = len(mids)
    tiles = total // (half * octet_count)
    piece = entered[0].shape[0]
    last = o == octet_count - 1

    def body(*refs):
        in_refs = refs[:GROUP]
        chunk_refs = refs[GROUP : GROUP + 4 * chunks]
        w_ref = refs[GROUP + 4 * chunks]
        ready_refs = refs[GROUP + 4 * chunks + 1 : -2]
        out_ref, state_s = refs[-2:]
        step = pl.program_id(0)

        @pl.when(step == 0)
        def _():
            place = my_place()
            for k in range(GROUP):
                state_s[place ^ k] = in_refs[k][...]

        def tile_of(c):
            mid_ref, z_ref, ag_ref, rr_ref = chunk_refs[4 * c : 4 * c + 4]
            read = spread_read(rr_ref[...].astype(F32), state)
            far = nn_dot(read, state_s[...].reshape(GROUP * piece, width))
            gated = (z_ref[...] + ag_ref[...].astype(F32) * far).astype(BF16)
            out = mid_ref[...] + nn_dot(gated, w_ref[...])
            if not last:
                out_ref[...] = out.astype(BF16)
                return
            cubes = [r[...].astype(F32) for r in ready_refs] + [out]
            cubes = [x.reshape(TILE_FRAMES, OCTET, width) for x in cubes]
            out_ref[...] = jnp.concatenate(cubes, axis=1).astype(BF16)

        for c in range(chunks):
            pl.when((step >= c * tiles) & (step < (c + 1) * tiles))(lambda c=c: tile_of(c))

    def own_tile(c, i):
        return jnp.clip(i - c * tiles, 0, tiles - 1)

    chunk_args, chunk_specs = [], []
    for c in range(chunks):
        chunk_args += [mids[c], *scanned[c]]
        chunk_specs.append(
            pl.BlockSpec((half, width), lambda i, c=c: (own_tile(c, i) * octet_count + o, 0))
        )
        chunk_specs += [
            pl.BlockSpec((half, cols), lambda i, c=c: (own_tile(c, i), 0))
            for cols in (width, width, LANES)
        ]
    octet_rows = pl.BlockSpec((half, width), lambda i: (i, 0))
    if last:
        out_spec = pl.BlockSpec((TILE_FRAMES, res, width), lambda i: (i, 0, 0))
        out_shape = jax.ShapeDtypeStruct((frames, res, width), BF16)
    else:
        out_spec = octet_rows
        out_shape = jax.ShapeDtypeStruct((chunks * tiles * half, width), BF16)
    return pl.pallas_call(
        body,
        grid=(chunks * tiles,),
        in_specs=[whole((piece, width))] * GROUP
        + chunk_specs
        + [whole(w_mix.shape)]
        + [octet_rows] * len(ready),
        out_specs=out_spec,
        out_shape=out_shape,
        scratch_shapes=[pltpu.VMEM((GROUP, piece, width), BF16)],
        compiler_params=grant(16),
        name="finish",
    )(*entered, *chunk_args, w_mix, *ready)


def local(
    tokens,
    cond_mask,
    cond_embed,
    attn_gain,
    w_qkv,
    w_out,
    mix_gain,
    w_in,
    decay_steps,
    segment_ids,
    skip_gain,
    w_mix_out,
):
    frames, res, width = tokens.shape
    heads = skip_gain.shape[0]
    state = (w_in.shape[1] - 2 * width) // 2
    tm_size = lax.axis_size("tm")
    peers = lax.axis_size("res")
    part = PART_FRAMES
    chunks = frames // (part * peers)
    order = list(range(peers - 1, 0, -1))

    def swap(value, k):
        return lax.ppermute(value, "res", [(i, i ^ k) for i in range(peers)])

    ids = segment_ids.reshape(-1, LANES)
    pieces = prepare(tokens, [], chunks, peers)
    gathered = []
    for c in range(chunks):
        mine = pieces[c * peers : (c + 1) * peers]
        got = {k: swap(mine[k], k) for k in order}
        got[0] = mine[0]
        gathered.append([got[k] for k in range(peers)])

    embed = cond_embed.reshape(-1, LANES)
    first_gain = attn_gain.reshape(-1, LANES)
    second_gain = mix_gain.reshape(-1, LANES)
    mixer_scale = 1.0 / math.sqrt(frames * tm_size * state)

    attended = []
    for c in range(chunks):
        outs = attend_chunk(
            cond_mask,
            gathered[c],
            embed,
            first_gain,
            w_qkv,
            c * part * peers,
            heads,
            [] if c else [decay_steps],
        )
        back = {k: swap(outs[k], k) for k in order}
        back[0] = outs[0]
        attended.append([back[k] for k in range(peers)])

    octet_count = res // OCTET

    def scan(o, c):
        _, mixed, entry, reach = held[c]
        return scan_octet(
            o, c, frames, ids, skip_gain, decay_steps, mixed, entry, reach, w_in, mixer_scale
        )

    carry, held, scanned = None, [], []
    for c in range(chunks):
        after = [rr for _, _, rr in scanned[-1]] if scanned else []
        out, carry = mix_chunk(
            c,
            chunks,
            cond_mask,
            ids,
            tokens,
            attended[c],
            decay_steps,
            embed,
            second_gain,
            w_out,
            w_in,
            carry,
            after,
        )
        held.append(out)
        scanned.append([scan(o, c) for o in range(octet_count)])
    covers = [rr for _, _, rr in scanned[-1]]
    entered = states_entering(carry, covers[:1], state, tm_size)
    mids = [mid for mid, _, _, _ in held]
    ready = []
    for o in range(octet_count):
        parts = [scanned[c][o] for c in range(chunks)]
        done = finish_octet(o, entered[o], mids, parts, w_mix_out, frames, res, state, ready)
        ready = ready + [done]
    return done


def solution(mesh):
    in_specs = (
        P("tm", "res", None),
        P("tm"),
        P(),
        P(),
        P(),
        P(),
        P(),
        P(),
        P("tm", "res", None),
        P(),
        P(),
        P(),
    )
    out_specs = P("tm", "res", None)
    return jax.shard_map(local, mesh=mesh, in_specs=in_specs, out_specs=out_specs, check_vma=False)
```

```python
import math

import jax
import jax.numpy as jnp
from jax import lax
from jax.experimental import pallas as pl
from jax.experimental.pallas import tpu as pltpu
from jax.sharding import PartitionSpec as P


BF16 = jnp.bfloat16
F32 = jnp.float32
LANES = 128
PART_FRAMES = 16
STAGE_FRAMES = 4
TILE_FRAMES = 32
OCTET = 8
GROUP = 4
CARRY_ROWS = 16


def rms_rows(rows, gain):
    mean = jnp.mean(rows * rows, axis=-1, keepdims=True)
    return rows * lax.rsqrt(mean + 1e-06) * gain


def nt_dot(a, b):
    return lax.dot_general(a, b, (((1,), (1,)), ((), ())), preferred_element_type=F32)


def tn_dot(a, b):
    return lax.dot_general(a, b, (((0,), (0,)), ((), ())), preferred_element_type=F32)


def nn_dot(a, b):
    return jnp.dot(a, b, preferred_element_type=F32)


def joined_row(ref):
    return jnp.concatenate([ref[i : i + 1] for i in range(ref.shape[0])], axis=1)


def first_reset(ids_ref, frames):
    ids = ids_ref[...]
    first = (ids == jnp.min(ids)).astype(F32)
    return jnp.sum(first).astype(jnp.int32) - lax.axis_index("tm") * frames


def my_place():
    return lax.axis_index("tm") % GROUP


def whole(shape):
    return pl.BlockSpec(shape, lambda i: (0,) * len(shape))


def grant(mib):
    return pltpu.CompilerParams(vmem_limit_bytes=mib << 20)


SMEM_SPEC = pl.BlockSpec(memory_space=pltpu.SMEM)
HBM_SPEC = pl.BlockSpec(memory_space=pl.ANY)


def prepare(tokens, after, chunks, peers):
    frames, res, width = tokens.shape
    part = frames // (chunks * peers)
    count = chunks * peers

    def body(*refs):
        tok_ref, out_refs = refs[0], refs[-count:]
        me = lax.axis_index("res")
        for c in range(chunks):
            for k in range(peers):
                start = c * part * peers + (me ^ k) * part
                out_refs[c * peers + k][...] = tok_ref[pl.ds(start, part)]

    piece = (part, res, width)
    return pl.pallas_call(
        body,
        grid=(1,),
        in_specs=[whole(tokens.shape)] + [HBM_SPEC] * len(after),
        out_specs=[whole(piece)] * count,
        out_shape=[jax.ShapeDtypeStruct(piece, tokens.dtype)] * count,
        compiler_params=grant(10),
        name="prepare",
    )(tokens, *after)


def attend_chunk(cond, parts, embed, gain, w_qkv, first_frame, heads, follow):
    peers = len(parts)
    frames, res, width = parts[0].shape
    head_size = width // heads
    keys = peers * res
    pairs = width // LANES
    inv_root = 1.0 / math.sqrt(head_size)

    def body(cond_ref, *refs):
        tok_refs = refs[:peers]
        embed_ref, gain_ref, w_ref = refs[peers : peers + 3]
        out_refs = refs[-peers - 2 : -2]
        norm_s, qkv_s = refs[-2:]
        me = lax.axis_index("res")
        embed_row = joined_row(embed_ref)
        gain_row = joined_row(gain_ref)
        for f in range(frames):
            flag = cond_ref[first_frame + me * frames + f].astype(F32)
            added = flag * embed_row
            for k in range(peers):
                rows = tok_refs[k][f].astype(F32) + added
                norm_s[k, f] = rms_rows(rows, gain_row).astype(BF16)
        flat = norm_s[...].reshape(peers * frames * res, width)
        shape = (peers, frames, res)
        got = nn_dot(flat, w_ref[:, : 2 * width]).astype(BF16)
        scaled = got[:, :width] * jnp.asarray(inv_root, BF16)
        qkv_s[:, :, :, :width] = scaled.reshape(*shape, width)
        qkv_s[:, :, :, width : 2 * width] = got[:, width:].reshape(*shape, width)
        got = nn_dot(flat, w_ref[:, 2 * width :]).astype(BF16)
        qkv_s[:, :, :, 2 * width :] = got.reshape(*shape, width)
        lane = lax.broadcasted_iota(jnp.int32, (1, LANES), 1)
        first = (lane < head_size).astype(BF16)
        second = (lane >= head_size).astype(BF16)
        pick = lax.broadcasted_iota(jnp.int32, (keys, LANES), 1) < head_size

        def stage(f0):
            units = [(f0 + f, p) for f in range(STAGE_FRAMES) for p in range(pairs)]

            def part(n, f, p):
                lo = n * width + p * LANES
                return qkv_s[:, pl.ds(f, 1), :, lo : lo + LANES].reshape(keys, LANES)

            scores = []
            for f, p in units:
                q = part(0, f, p)
                stacked = jnp.concatenate([q * first, q * second], axis=0)
                scores.append(nt_dot(part(1, f, p), stacked))
            tops = [jnp.max(x, axis=0, keepdims=True) for x in scores]
            weights = [jnp.exp(x - t) for x, t in zip(scores, tops)]
            totals = [jnp.sum(w, axis=0, keepdims=True) for w in weights]
            weights = [(w * (1.0 / t)).astype(BF16) for w, t in zip(weights, totals)]
            both = [tn_dot(w, part(2, f, p)) for w, (f, p) in zip(weights, units)]
            for got, (f, p) in zip(both, units):
                att = jnp.where(pick, got[:keys], got[keys:]).astype(BF16)
                for k in range(peers):
                    out_refs[k][pl.ds(f, 1), :, p * LANES : (p + 1) * LANES] = att[
                        k * res : (k + 1) * res
                    ].reshape(1, res, LANES)

        def step(i, _):
            stage(i * STAGE_FRAMES)
            return 0

        lax.fori_loop(0, frames // STAGE_FRAMES, step, 0)

    block = whole((frames, res, width))
    return pl.pallas_call(
        body,
        grid=(1,),
        in_specs=[SMEM_SPEC]
        + [block] * peers
        + [whole(a.shape) for a in (embed, gain, w_qkv)]
        + [HBM_SPEC] * len(follow),
        out_specs=[block] * peers,
        out_shape=[jax.ShapeDtypeStruct((frames, res, width), BF16)] * peers,
        scratch_shapes=[
            pltpu.VMEM((peers, frames, res, width), BF16),
            pltpu.VMEM((peers, frames, res, 3 * width), BF16),
        ],
        compiler_params=grant(14),
        name="attend",
    )(cond, *parts, embed, gain, w_qkv, *follow)


def octets(rows, frames, res):
    n = rows.shape[-1]
    cube = rows.reshape(frames, res, n)
    return [
        cube[:, o * OCTET : (o + 1) * OCTET].reshape(frames * OCTET, n) for o in range(res // OCTET)
    ]


def wide_decays(steps, heads, width):
    values = 1.0 - steps.astype(F32) * (1.0 / 4096.0)
    rows = values.shape[0]
    head_size = width // heads
    per = LANES // head_size
    lane_head = lax.broadcasted_iota(jnp.int32, (rows, LANES), 1) // head_size
    parts = []
    for p in range(width // LANES):
        part = jnp.broadcast_to(values[:, p * per : p * per + 1], (rows, LANES))
        for h in range(1, per):
            col = values[:, p * per + h : p * per + h + 1]
            part = jnp.where(lane_head == h, jnp.broadcast_to(col, (rows, LANES)), part)
        parts.append(part)
    return jnp.concatenate(parts, axis=1)


def frame_rows(value, f):
    return value[f * OCTET : (f + 1) * OCTET]


def twice_each(maps, state):
    low = lax.broadcasted_iota(jnp.int32, maps.shape, 1) < state
    turned = pltpu.roll(maps, state, 1)
    return jnp.where(low, maps, turned), jnp.where(low, turned, maps)


def spread_read(rr, state):
    rows = rr.shape[0]
    mine = lax.broadcasted_iota(jnp.int32, (rows, LANES), 0) % OCTET
    lane = lax.broadcasted_iota(jnp.int32, (rows, LANES), 1) // state
    per = LANES // state
    return jnp.concatenate(
        [jnp.where(mine - j * per == lane, rr, 0.0).astype(BF16) for j in range(OCTET // per)],
        axis=1,
    )


def mix_chunk(c, chunks, cond, ids, tokens, attended, steps, embed, gain, w_out, w_in, carry, follow):
    frames_all, res, width = tokens.shape
    heads = steps.shape[-1]
    peers = len(attended)
    part_frames = attended[0].shape[0]
    frames = part_frames * peers
    tiles = frames // TILE_FRAMES
    rows = TILE_FRAMES * res
    half = TILE_FRAMES * OCTET
    mixed_width = w_in.shape[1]
    state = (mixed_width - 2 * width) // 2
    spread = res * state
    last = c == chunks - 1
    pays = GROUP * (res // OCTET)
    per_pay = OCTET // GROUP
    pay_rows = per_pay * state
    carry_args = [] if carry is None else list(carry)
    n_in = 8 + peers

    def body(*refs):
        cond_ref, ids_ref, tok_ref = refs[:3]
        att_refs = refs[3 : 3 + peers]
        steps_ref, embed_ref, gain_ref, wo_ref, wi_ref = refs[3 + peers : n_in]
        pos = n_in + len(carry_args)
        carry_refs = refs[n_in:pos]
        pos += len(follow)
        mid_ref, mixed_ref, entry_ref, reach_ref = refs[pos : pos + 4]
        pos += 4
        pay_refs = refs[pos : pos + pays] if last else ()
        pos += len(pay_refs)
        if last:
            att_s, s_ref, p_ref, p_wide = refs[pos:]
        else:
            s_ref, p_ref, att_s = refs[pos:]
        reset = first_reset(ids_ref, frames_all)
        me, place = lax.axis_index("res"), my_place()
        for k in range(peers):
            att_s[me ^ k] = att_refs[k][...]
        if carry is None:
            s_ref[...] = jnp.zeros_like(s_ref)
            p_ref[...] = jnp.ones_like(p_ref)
        else:
            s_ref[...] = carry_refs[0][...]
            p_ref[...] = carry_refs[1][...]
        embed_row = joined_row(embed_ref)
        gain_row = joined_row(gain_ref)
        att_all = att_s[...].reshape(frames * res, width)
        for i in range(tiles):
            g0 = c * frames + i * TILE_FRAMES
            g_end = g0 + TILE_FRAMES - 1
            sl = slice(i * rows, (i + 1) * rows)
            hidden = jnp.concatenate(
                [
                    tok_ref[i * TILE_FRAMES + f].astype(F32)
                    + cond_ref[g0 + f].astype(F32) * embed_row
                    for f in range(TILE_FRAMES)
                ],
                axis=0,
            )
            mid = hidden + nn_dot(att_all[sl], wo_ref[...])
            mid_ref[sl] = jnp.concatenate(octets(mid, TILE_FRAMES, res), axis=0)
            mixer_in = rms_rows(mid, gain_row)
            mixer_in = jnp.concatenate(octets(mixer_in, TILE_FRAMES, res), axis=0).astype(BF16)
            mixed_ref[sl, width:] = nn_dot(mixer_in, wi_ref[:, width:]).astype(BF16)
            mixed_ref[sl, :width] = mixer_in
            tile_steps = steps_ref[i * TILE_FRAMES : (i + 1) * TILE_FRAMES]
            keep_end = [
                jnp.where((reset > g0 + f) & (reset <= g_end), 0.0, 1.0).astype(F32)
                for f in range(TILE_FRAMES)
            ]
            keep_all = jnp.where((reset >= g0) & (reset <= g_end), 0.0, 1.0).astype(F32)
            entry_ref[i] = s_ref[...].astype(BF16)
            reach_ref[i] = p_ref[...]
            for o in range(res // OCTET):
                os = slice(i * rows + o * half, i * rows + (o + 1) * half)
                st = tile_steps[:, o * OCTET : (o + 1) * OCTET].reshape(half, heads)
                decay = wide_decays(st, heads, width)
                after = [jnp.ones((OCTET, width), F32)]
                for f in range(TILE_FRAMES - 1, 0, -1):
                    after.append(after[-1] * frame_rows(decay, f))
                transit = after[-1] * frame_rows(decay, 0) * keep_all
                after = after[::-1]
                kept = jnp.concatenate([a * s for a, s in zip(after, keep_end)], axis=0)
                inner = mixed_ref[os, width : 2 * width].astype(F32)
                kept = (inner * kept).astype(BF16)
                maps = mixed_ref[os, 2 * width :].astype(F32)
                write_t = maps.T[:state]
                col = lax.broadcasted_iota(jnp.int32, (state, half), 1) % OCTET
                write = jnp.concatenate(
                    [jnp.where(col == r, write_t, 0.0).astype(BF16) for r in range(OCTET)], axis=0
                )
                added = nn_dot(write, kept)
                for r in range(OCTET):
                    rs = slice(r * state, (r + 1) * state)
                    ss = slice((o * OCTET + r) * state, (o * OCTET + r + 1) * state)
                    s_ref[ss] = s_ref[ss] * transit[r : r + 1] + added[rs]
                po = slice(o * OCTET, (o + 1) * OCTET)
                p_ref[po] = p_ref[po] * transit
        if not last:
            return
        p_all = p_ref[...]
        for r in range(res):
            p_wide[r] = jnp.broadcast_to(p_all[r : r + 1], (8, width))
        sub = lax.broadcasted_iota(jnp.int32, (CARRY_ROWS, width), 0) % 8
        for e in range(res // OCTET):
            for k in range(GROUP):
                r0 = e * OCTET + (place ^ k) * per_pay
                out = pay_refs[e * GROUP + k]
                start = pl.multiple_of(r0 * state, pay_rows)
                out[:pay_rows] = s_ref[pl.ds(start, pay_rows), :].astype(BF16)
                for n in range(0, per_pay, 2):
                    value = jnp.concatenate([p_wide[r0 + n], p_wide[r0 + n + 1]], axis=0)
                    upper = value.astype(BF16).astype(F32)
                    lo = pay_rows + n * 8
                    out[lo : lo + 16] = jnp.where(sub < 4, upper, value - upper).astype(BF16)

    chunk_rows = frames * res
    in_specs = (
        [SMEM_SPEC, whole(ids.shape)]
        + [pl.BlockSpec((frames, res, width), lambda i: (c, 0, 0))]
        + [whole(attended[0].shape)] * peers
        + [pl.BlockSpec((frames, res, heads), lambda i: (c, 0, 0))]
        + [whole(a.shape) for a in (embed, gain, w_out, w_in)]
        + [whole(a.shape) for a in carry_args]
        + [HBM_SPEC] * len(follow)
    )
    out_shape = [
        jax.ShapeDtypeStruct((chunk_rows, width), F32),
        jax.ShapeDtypeStruct((chunk_rows, mixed_width), BF16),
        jax.ShapeDtypeStruct((tiles, spread, width), BF16),
        jax.ShapeDtypeStruct((tiles, res, width), F32),
    ]
    scratch = [pltpu.VMEM((peers, part_frames, res, width), BF16)]
    if last:
        pay = (pay_rows + 8 * per_pay, width)
        out_shape += [jax.ShapeDtypeStruct(pay, BF16)] * pays
        scratch += [
            pltpu.VMEM((spread, width), F32),
            pltpu.VMEM((res, width), F32),
            pltpu.VMEM((res, 8, width), F32),
        ]
    else:
        out_shape += [
            jax.ShapeDtypeStruct((spread, width), F32),
            jax.ShapeDtypeStruct((res, width), F32),
        ]
    outs = pl.pallas_call(
        body,
        grid=(1,),
        in_specs=in_specs,
        out_specs=[whole(o.shape) for o in out_shape],
        out_shape=out_shape,
        scratch_shapes=scratch,
        compiler_params=grant(20),
        name="mix",
    )(cond, ids, tokens, *attended, steps, embed, gain, w_out, w_in, *carry_args, *follow)
    return outs[:4], outs[4:]


def scan_octet(o, c, frames_all, ids, skip, steps, mixed, entry, reach, w_in, mixer_scale):
    tiles, spread, width = entry.shape
    _, res, heads = steps.shape
    state = spread // res
    half = TILE_FRAMES * OCTET
    octet_state = OCTET * state
    octet_count = res // OCTET

    def body(
        ids_ref,
        skip_ref,
        steps_ref,
        mixed_ref,
        entry_ref,
        reach_ref,
        wg_ref,
        z_ref,
        ag_ref,
        rr_ref,
    ):
        reset = first_reset(ids_ref, frames_all)
        feature = lax.broadcasted_iota(jnp.int32, (1, width), 1) // (width // heads)
        skip_row = jnp.zeros((1, width), F32)
        for h in range(heads):
            skip_row = jnp.where(feature == h, skip_ref[h], skip_row)
        g0 = c * tiles * TILE_FRAMES + pl.program_id(0) * TILE_FRAMES
        row_i = lax.broadcasted_iota(jnp.int32, (half, half), 0)
        col_i = lax.broadcasted_iota(jnp.int32, (half, half), 1)
        edge = (reset - g0) * OCTET
        joined = (
            ((row_i % OCTET) == (col_i % OCTET))
            & (row_i >= col_i)
            & ((row_i >= edge) == (col_i >= edge))
        )
        keep_start = [
            jnp.where((reset >= g0) & (reset <= g0 + f), 0.0, 1.0).astype(F32)
            for f in range(TILE_FRAMES)
        ]
        decay = wide_decays(steps_ref[...].reshape(half, heads), heads, width)
        before = [frame_rows(decay, 0)]
        for f in range(1, TILE_FRAMES):
            before.append(before[-1] * frame_rows(decay, f))
        after = [jnp.ones((OCTET, width), F32)]
        for f in range(TILE_FRAMES - 1, 0, -1):
            after.append(after[-1] * frame_rows(decay, f))
        after = jnp.concatenate(after[::-1], axis=0)
        back = 1.0 / before[-1]
        relative = jnp.concatenate([b * back for b in before], axis=0)
        from_base = jnp.concatenate([b * s for b, s in zip(before, keep_start)], axis=0)
        inner = mixed_ref[:, width : 2 * width].astype(F32)
        ww, rr = twice_each(mixed_ref[:, 2 * width :].astype(F32), state)
        rr_ref[...] = rr.astype(BF16)
        gram = nt_dot(rr.astype(BF16), ww.astype(BF16)) * 0.5
        gram = jnp.where(joined, gram, 0.0).astype(BF16)
        near = nn_dot(gram, (inner * after).astype(BF16)) * relative
        far = nn_dot(spread_read(rr, state), entry_ref[0]) * from_base
        gate = nn_dot(mixed_ref[:, :width], wg_ref[...]).astype(BF16).astype(F32)
        gate = 0.5 * gate
        silu = gate + gate * jnp.tanh(gate)
        z_ref[...] = ((near + far) * mixer_scale + skip_row * inner) * silu
        start = reach_ref[0] * mixer_scale
        reached = jnp.concatenate(
            [start * frame_rows(from_base, f) for f in range(TILE_FRAMES)], axis=0
        )
        ag_ref[...] = (reached * silu).astype(BF16)

    total = tiles * half

    def row_block(cols):
        return pl.BlockSpec((half, cols), lambda i: (i, 0))

    return pl.pallas_call(
        body,
        grid=(tiles,),
        in_specs=[
            whole(ids.shape),
            SMEM_SPEC,
            pl.BlockSpec((TILE_FRAMES, OCTET, heads), lambda i: (c * tiles + i, o, 0)),
            pl.BlockSpec((half, mixed.shape[1]), lambda i: (i * octet_count + o, 0)),
            pl.BlockSpec((1, octet_state, width), lambda i: (i, o, 0)),
            pl.BlockSpec((1, OCTET, width), lambda i: (i, o, 0)),
            whole((width, width)),
        ],
        out_specs=[row_block(width), row_block(width), row_block(LANES)],
        out_shape=[
            jax.ShapeDtypeStruct((total, width), F32),
            jax.ShapeDtypeStruct((total, width), BF16),
            jax.ShapeDtypeStruct((total, LANES), BF16),
        ],
        compiler_params=grant(14),
        name="scan",
    )(ids, skip, steps, mixed, entry, reach, w_in)


def decay_rows(tail, n):
    tail = tail.astype(F32)
    return [tail[8 * i : 8 * i + 1] + tail[8 * i + 4 : 8 * i + 5] for i in range(n)]


def residues_of(pay, state):
    return pay // (state + 8)


def group_total(got, after, state):
    pay, width = got[0].shape
    n = residues_of(pay, state)
    body_rows = n * state

    def body(*refs):
        got_refs = refs[:GROUP]
        out_ref, sorted_s = refs[-2:]
        place = my_place()
        for k in range(GROUP):
            sorted_s[place ^ k] = got_refs[k][...]
        tails = [decay_rows(sorted_s[j, body_rows:], n) for j in range(GROUP)]
        sub = lax.broadcasted_iota(jnp.int32, (CARRY_ROWS, width), 0) % 8
        lines = []
        for i in range(n):
            rs = slice(i * state, (i + 1) * state)
            total = sorted_s[0, rs].astype(F32)
            product = tails[0][i]
            for j in range(1, GROUP):
                total = total * tails[j][i] + sorted_s[j, rs].astype(F32)
                product = product * tails[j][i]
            out_ref[rs] = total.astype(BF16)
            lines.append(jnp.broadcast_to(product, (8, width)))
        for i in range(0, n, 2):
            value = jnp.concatenate(lines[i : i + 2], axis=0)
            upper = value.astype(BF16).astype(F32)
            lo = body_rows + 8 * i
            out_ref[lo : lo + 16] = jnp.where(sub < 4, upper, value - upper).astype(BF16)

    return pl.pallas_call(
        body,
        grid=(1,),
        in_specs=[whole((pay, width))] * GROUP + [HBM_SPEC] * len(after),
        out_specs=whole((pay, width)),
        out_shape=jax.ShapeDtypeStruct((pay, width), BF16),
        scratch_shapes=[pltpu.VMEM((GROUP, pay, width), BF16)],
        compiler_params=grant(6),
        name="group_total",
    )(*got, *after)


def group_prefixes(got, entering, after, state):
    pay, width = got[0].shape
    n = residues_of(pay, state)
    body_rows = n * state

    def body(*refs):
        got_refs, in_ref = refs[:GROUP], refs[GROUP]
        out_refs = refs[-GROUP - 2 : -2]
        sorted_s, prefix_s = refs[-2:]
        place = my_place()
        for k in range(GROUP):
            sorted_s[place ^ k] = got_refs[k][...]
        tails = [decay_rows(sorted_s[j, body_rows:], n) for j in range(GROUP)]
        for i in range(n):
            rs = slice(i * state, (i + 1) * state)
            total = in_ref[rs].astype(F32)
            prefix_s[0, rs] = total.astype(BF16)
            for j in range(GROUP - 1):
                total = total * tails[j][i] + sorted_s[j, rs].astype(F32)
                prefix_s[j + 1, rs] = total.astype(BF16)
        for k in range(GROUP):
            out_refs[k][...] = prefix_s[place ^ k]

    spec = whole((pay, width))
    out = whole((body_rows, width))
    return pl.pallas_call(
        body,
        grid=(1,),
        in_specs=[spec] * (GROUP + 1) + [HBM_SPEC] * len(after),
        out_specs=[out] * GROUP,
        out_shape=[jax.ShapeDtypeStruct((body_rows, width), BF16)] * GROUP,
        scratch_shapes=[
            pltpu.VMEM((GROUP, pay, width), BF16),
            pltpu.VMEM((GROUP, body_rows, width), BF16),
        ],
        compiler_params=grant(8),
        name="group_prefixes",
    )(*got, entering, *after)


def join_payloads(earlier, later, state):
    n = residues_of(later.shape[0], state)
    body_rows = n * state
    width = later.shape[1]
    early = decay_rows(earlier[body_rows:], n)
    late = decay_rows(later[body_rows:], n)
    parts, lines = [], []
    for i in range(n):
        rs = slice(i * state, (i + 1) * state)
        parts.append(earlier[rs].astype(F32) * late[i] + later[rs].astype(F32))
        value = early[i] * late[i]
        upper = value.astype(BF16).astype(F32)
        lines += [jnp.broadcast_to(upper, (4, width)), jnp.broadcast_to(value - upper, (4, width))]
    return jnp.concatenate(parts + lines, axis=0).astype(BF16)


def states_entering(payloads, covers, state, tm_size):
    groups = tm_size // GROUP
    order = list(range(GROUP - 1, 0, -1))

    def swap(parts):
        moved = {
            k: lax.ppermute(parts[k], "tm", [(i, i ^ k) for i in range(tm_size)]) for k in order
        }
        return [parts[0]] + [moved[k] for k in range(1, GROUP)]

    def onward(value, hops):
        moved = hops * GROUP
        return lax.ppermute(value, "tm", [(i, i + moved) for i in range(tm_size - moved)])

    octet_count = len(payloads) // GROUP
    gathered = [swap(payloads[e * GROUP : (e + 1) * GROUP]) for e in range(octet_count)]
    result = []
    for e, got in enumerate(gathered):
        total = group_total(got, covers[e : e + 1], state)
        entering = onward(total, 1) if groups > 1 else jnp.zeros_like(total)
        hops = 1
        while hops < groups - 1:
            entering = join_payloads(onward(entering, hops), entering, state)
            hops *= 2
        result.append(swap(group_prefixes(got, entering, [], state)))
    return result


def finish_octet(o, entered, mids, scanned, w_mix, frames, res, state, ready):
    total, width = mids[0].shape
    octet_count = res // OCTET
    half = TILE_FRAMES * OCTET
    chunks = len(mids)
    tiles = total // (half * octet_count)
    rows = tiles * half
    piece = entered[0].shape[0]
    last = o == octet_count - 1

    def body(*refs):
        in_refs = refs[:GROUP]
        chunk_refs = refs[GROUP : GROUP + 4 * chunks]
        w_ref = refs[GROUP + 4 * chunks]
        ready_refs = refs[GROUP + 4 * chunks + 1 : -2]
        out_ref, state_s = refs[-2:]
        step = pl.program_id(0)

        @pl.when(step == 0)
        def _():
            place = my_place()
            for k in range(GROUP):
                state_s[place ^ k] = in_refs[k][...]

        def tile_of(c):
            mid_ref, z_ref, ag_ref, rr_ref = chunk_refs[4 * c : 4 * c + 4]
            read = spread_read(rr_ref[...].astype(F32), state)
            far = nn_dot(read, state_s[...].reshape(GROUP * piece, width))
            gated = (z_ref[...] + ag_ref[...].astype(F32) * far).astype(BF16)
            out = mid_ref[...].reshape(rows, width) + nn_dot(gated, w_ref[...])
            if not last:
                out_ref[...] = out.astype(BF16)
                return
            cubes = [r[...].astype(F32) for r in ready_refs] + [out]
            cubes = [x.reshape(tiles * TILE_FRAMES, OCTET, width) for x in cubes]
            out_ref[...] = jnp.concatenate(cubes, axis=1).astype(BF16)

        for c in range(chunks):
            pl.when(step == c)(lambda c=c: tile_of(c))

    chunk_args, chunk_specs = [], []
    for c in range(chunks):
        chunk_args += [mids[c].reshape(tiles, octet_count, half, width), *scanned[c]]
        chunk_specs.append(pl.BlockSpec((tiles, 1, half, width), lambda i: (0, o, 0, 0)))
        chunk_specs += [whole((rows, cols)) for cols in (width, width, LANES)]
    octet_rows = pl.BlockSpec((rows, width), lambda i: (i, 0))
    if last:
        out_spec = pl.BlockSpec((tiles * TILE_FRAMES, res, width), lambda i: (i, 0, 0))
        out_shape = jax.ShapeDtypeStruct((frames, res, width), BF16)
    else:
        out_spec = octet_rows
        out_shape = jax.ShapeDtypeStruct((chunks * rows, width), BF16)
    return pl.pallas_call(
        body,
        grid=(chunks,),
        in_specs=[whole((piece, width))] * GROUP
        + chunk_specs
        + [whole(w_mix.shape)]
        + [octet_rows] * len(ready),
        out_specs=out_spec,
        out_shape=out_shape,
        scratch_shapes=[pltpu.VMEM((GROUP, piece, width), BF16)],
        compiler_params=grant(20),
        name="finish",
    )(*entered, *chunk_args, w_mix, *ready)


def local(
    tokens,
    cond_mask,
    cond_embed,
    attn_gain,
    w_qkv,
    w_out,
    mix_gain,
    w_in,
    decay_steps,
    segment_ids,
    skip_gain,
    w_mix_out,
):
    frames, res, width = tokens.shape
    heads = skip_gain.shape[0]
    state = (w_in.shape[1] - 2 * width) // 2
    tm_size = lax.axis_size("tm")
    peers = lax.axis_size("res")
    part = PART_FRAMES
    chunks = frames // (part * peers)
    order = list(range(peers - 1, 0, -1))

    def swap(value, k):
        return lax.ppermute(value, "res", [(i, i ^ k) for i in range(peers)])

    ids = segment_ids.reshape(-1, LANES)
    pieces = prepare(tokens, [], chunks, peers)
    gathered = []
    for c in range(chunks):
        mine = pieces[c * peers : (c + 1) * peers]
        got = {k: swap(mine[k], k) for k in order}
        got[0] = mine[0]
        gathered.append([got[k] for k in range(peers)])

    embed = cond_embed.reshape(-1, LANES)
    first_gain = attn_gain.reshape(-1, LANES)
    second_gain = mix_gain.reshape(-1, LANES)
    mixer_scale = 1.0 / math.sqrt(frames * tm_size * state)

    attended = []
    for c in range(chunks):
        outs = attend_chunk(
            cond_mask,
            gathered[c],
            embed,
            first_gain,
            w_qkv,
            c * part * peers,
            heads,
            [] if c else [decay_steps],
        )
        back = {k: swap(outs[k], k) for k in order}
        back[0] = outs[0]
        attended.append([back[k] for k in range(peers)])

    octet_count = res // OCTET

    def scan(o, c):
        _, mixed, entry, reach = held[c]
        return scan_octet(
            o, c, frames, ids, skip_gain, decay_steps, mixed, entry, reach, w_in, mixer_scale
        )

    carry, held, scanned = None, [], []
    for c in range(chunks):
        after = [scanned[-1][0][2]] if scanned else []
        out, carry = mix_chunk(
            c,
            chunks,
            cond_mask,
            ids,
            tokens,
            attended[c],
            decay_steps,
            embed,
            second_gain,
            w_out,
            w_in,
            carry,
            after,
        )
        held.append(out)
        scanned.append([scan(o, c) for o in range(octet_count)])
    covers = [scanned[-1][0][2], scanned[0][-1][2]]
    entered = states_entering(carry, covers, state, tm_size)
    mids = [mid for mid, _, _, _ in held]
    ready = []
    for o in range(octet_count):
        parts = [scanned[c][o] for c in range(chunks)]
        done = finish_octet(o, entered[o], mids, parts, w_mix_out, frames, res, state, ready)
        ready = ready + [done]
    return done


def solution(mesh):
    in_specs = (
        P("tm", "res", None),
        P("tm"),
        P(),
        P(),
        P(),
        P(),
        P(),
        P(),
        P("tm", "res", None),
        P(),
        P(),
        P(),
    )
    out_specs = P("tm", "res", None)
    return jax.shard_map(local, mesh=mesh, in_specs=in_specs, out_specs=out_specs, check_vma=False)
```

```python
import math

import jax
import jax.numpy as jnp
from jax import lax
from jax.experimental import pallas as pl
from jax.experimental.pallas import tpu as pltpu
from jax.sharding import PartitionSpec as P


BF16 = jnp.bfloat16
F32 = jnp.float32
LANES = 128
PART_FRAMES = 16
STAGE_FRAMES = 8
TILE_FRAMES = 32
OCTET = 8
GROUP = 4
CARRY_ROWS = 16


def rms_rows(rows, gain):
    mean = jnp.mean(rows * rows, axis=-1, keepdims=True)
    return rows * lax.rsqrt(mean + 1e-06) * gain


def nt_dot(a, b):
    return lax.dot_general(a, b, (((1,), (1,)), ((), ())), preferred_element_type=F32)


def tn_dot(a, b):
    return lax.dot_general(a, b, (((0,), (0,)), ((), ())), preferred_element_type=F32)


def nn_dot(a, b):
    return jnp.dot(a, b, preferred_element_type=F32)


def joined_row(ref):
    return jnp.concatenate([ref[i : i + 1] for i in range(ref.shape[0])], axis=1)


def first_reset(ids_ref, frames):
    ids = ids_ref[...]
    first = (ids == jnp.min(ids)).astype(F32)
    return jnp.sum(first).astype(jnp.int32) - lax.axis_index("tm") * frames


def my_place():
    return lax.axis_index("tm") % GROUP


def whole(shape):
    return pl.BlockSpec(shape, lambda i: (0,) * len(shape))


def grant(mib):
    return pltpu.CompilerParams(vmem_limit_bytes=mib << 20)


SMEM_SPEC = pl.BlockSpec(memory_space=pltpu.SMEM)
HBM_SPEC = pl.BlockSpec(memory_space=pl.ANY)


def prepare(tokens, after, chunks, peers):
    frames, res, width = tokens.shape
    part = frames // (chunks * peers)
    count = chunks * peers

    def body(*refs):
        tok_ref, out_refs = refs[0], refs[-count:]
        me = lax.axis_index("res")
        for c in range(chunks):
            for k in range(peers):
                start = c * part * peers + (me ^ k) * part
                out_refs[c * peers + k][...] = tok_ref[pl.ds(start, part)]

    piece = (part, res, width)
    return pl.pallas_call(
        body,
        grid=(1,),
        in_specs=[whole(tokens.shape)] + [HBM_SPEC] * len(after),
        out_specs=[whole(piece)] * count,
        out_shape=[jax.ShapeDtypeStruct(piece, tokens.dtype)] * count,
        compiler_params=grant(10),
        name="prepare",
    )(tokens, *after)


def attend_chunk(cond, parts, embed, gain, w_qkv, first_frame, heads, follow):
    peers = len(parts)
    frames, res, width = parts[0].shape
    head_size = width // heads
    keys = peers * res
    pairs = width // LANES
    inv_root = 1.0 / math.sqrt(head_size)

    def body(cond_ref, *refs):
        tok_refs = refs[:peers]
        embed_ref, gain_ref, w_ref = refs[peers : peers + 3]
        out_refs = refs[-peers - 2 : -2]
        norm_s, qkv_s = refs[-2:]
        me = lax.axis_index("res")
        embed_row = joined_row(embed_ref)
        gain_row = joined_row(gain_ref)
        for f in range(frames):
            flag = cond_ref[first_frame + me * frames + f].astype(F32)
            added = flag * embed_row
            for k in range(peers):
                rows = tok_refs[k][f].astype(F32) + added
                norm_s[k, f] = rms_rows(rows, gain_row).astype(BF16)
        flat = norm_s[...].reshape(peers * frames * res, width)
        shape = (peers, frames, res)
        got = nn_dot(flat, w_ref[:, : 2 * width]).astype(BF16)
        scaled = got[:, :width] * jnp.asarray(inv_root, BF16)
        qkv_s[:, :, :, :width] = scaled.reshape(*shape, width)
        qkv_s[:, :, :, width : 2 * width] = got[:, width:].reshape(*shape, width)
        got = nn_dot(flat, w_ref[:, 2 * width :]).astype(BF16)
        qkv_s[:, :, :, 2 * width :] = got.reshape(*shape, width)
        lane = lax.broadcasted_iota(jnp.int32, (1, LANES), 1)
        first = (lane < head_size).astype(BF16)
        second = (lane >= head_size).astype(BF16)
        pick = lax.broadcasted_iota(jnp.int32, (keys, LANES), 1) < head_size

        def stage(f0):
            units = [(f0 + f, p) for f in range(STAGE_FRAMES) for p in range(pairs)]

            def part(n, f, p):
                lo = n * width + p * LANES
                return qkv_s[:, pl.ds(f, 1), :, lo : lo + LANES].reshape(keys, LANES)

            scores = []
            for f, p in units:
                q = part(0, f, p)
                stacked = jnp.concatenate([q * first, q * second], axis=0)
                scores.append(nt_dot(part(1, f, p), stacked))
            tops = [jnp.max(x, axis=0, keepdims=True) for x in scores]
            weights = [jnp.exp(x - t) for x, t in zip(scores, tops)]
            totals = [jnp.sum(w, axis=0, keepdims=True) for w in weights]
            weights = [(w * (1.0 / t)).astype(BF16) for w, t in zip(weights, totals)]
            both = [tn_dot(w, part(2, f, p)) for w, (f, p) in zip(weights, units)]
            for got, (f, p) in zip(both, units):
                att = jnp.where(pick, got[:keys], got[keys:]).astype(BF16)
                for k in range(peers):
                    out_refs[k][pl.ds(f, 1), :, p * LANES : (p + 1) * LANES] = att[
                        k * res : (k + 1) * res
                    ].reshape(1, res, LANES)

        def step(i, _):
            stage(i * STAGE_FRAMES)
            return 0

        lax.fori_loop(0, frames // STAGE_FRAMES, step, 0)

    block = whole((frames, res, width))
    return pl.pallas_call(
        body,
        grid=(1,),
        in_specs=[SMEM_SPEC]
        + [block] * peers
        + [whole(a.shape) for a in (embed, gain, w_qkv)]
        + [HBM_SPEC] * len(follow),
        out_specs=[block] * peers,
        out_shape=[jax.ShapeDtypeStruct((frames, res, width), BF16)] * peers,
        scratch_shapes=[
            pltpu.VMEM((peers, frames, res, width), BF16),
            pltpu.VMEM((peers, frames, res, 3 * width), BF16),
        ],
        compiler_params=grant(14),
        name="attend",
    )(cond, *parts, embed, gain, w_qkv, *follow)


def octets(rows, frames, res):
    n = rows.shape[-1]
    cube = rows.reshape(frames, res, n)
    return [
        cube[:, o * OCTET : (o + 1) * OCTET].reshape(frames * OCTET, n) for o in range(res // OCTET)
    ]


def wide_decays(steps, heads, width):
    values = 1.0 - steps.astype(F32) * (1.0 / 4096.0)
    rows = values.shape[0]
    head_size = width // heads
    per = LANES // head_size
    lane_head = lax.broadcasted_iota(jnp.int32, (rows, LANES), 1) // head_size
    parts = []
    for p in range(width // LANES):
        part = jnp.broadcast_to(values[:, p * per : p * per + 1], (rows, LANES))
        for h in range(1, per):
            col = values[:, p * per + h : p * per + h + 1]
            part = jnp.where(lane_head == h, jnp.broadcast_to(col, (rows, LANES)), part)
        parts.append(part)
    return jnp.concatenate(parts, axis=1)


def frame_rows(value, f):
    return value[f * OCTET : (f + 1) * OCTET]


def twice_each(maps, state):
    low = lax.broadcasted_iota(jnp.int32, maps.shape, 1) < state
    turned = pltpu.roll(maps, state, 1)
    return jnp.where(low, maps, turned), jnp.where(low, turned, maps)


def spread_read(rr, state):
    rows = rr.shape[0]
    mine = lax.broadcasted_iota(jnp.int32, (rows, LANES), 0) % OCTET
    lane = lax.broadcasted_iota(jnp.int32, (rows, LANES), 1) // state
    per = LANES // state
    return jnp.concatenate(
        [jnp.where(mine - j * per == lane, rr, 0.0).astype(BF16) for j in range(OCTET // per)],
        axis=1,
    )


def mix_chunk(c, chunks, cond, ids, tokens, attended, steps, embed, gain, w_out, w_in, carry, follow):
    frames_all, res, width = tokens.shape
    heads = steps.shape[-1]
    peers = len(attended)
    part_frames = attended[0].shape[0]
    frames = part_frames * peers
    tiles = frames // TILE_FRAMES
    rows = TILE_FRAMES * res
    half = TILE_FRAMES * OCTET
    mixed_width = w_in.shape[1]
    state = (mixed_width - 2 * width) // 2
    spread = res * state
    last = c == chunks - 1
    pays = GROUP * (res // OCTET)
    per_pay = OCTET // GROUP
    pay_rows = per_pay * state
    carry_args = [] if carry is None else list(carry)
    n_in = 8 + peers

    def body(*refs):
        cond_ref, ids_ref, tok_ref = refs[:3]
        att_refs = refs[3 : 3 + peers]
        steps_ref, embed_ref, gain_ref, wo_ref, wi_ref = refs[3 + peers : n_in]
        pos = n_in + len(carry_args)
        carry_refs = refs[n_in:pos]
        pos += len(follow)
        mid_ref, mixed_ref, entry_ref, reach_ref = refs[pos : pos + 4]
        pos += 4
        pay_refs = refs[pos : pos + pays] if last else ()
        pos += len(pay_refs)
        if last:
            att_s, s_ref, p_ref, p_wide = refs[pos:]
        else:
            s_ref, p_ref, att_s = refs[pos:]
        reset = first_reset(ids_ref, frames_all)
        me, place = lax.axis_index("res"), my_place()
        for k in range(peers):
            att_s[me ^ k] = att_refs[k][...]
        if carry is None:
            s_ref[...] = jnp.zeros_like(s_ref)
            p_ref[...] = jnp.ones_like(p_ref)
        else:
            s_ref[...] = carry_refs[0][...]
            p_ref[...] = carry_refs[1][...]
        embed_row = joined_row(embed_ref)
        gain_row = joined_row(gain_ref)
        att_all = att_s[...].reshape(frames * res, width)
        for i in range(tiles):
            g0 = c * frames + i * TILE_FRAMES
            g_end = g0 + TILE_FRAMES - 1
            sl = slice(i * rows, (i + 1) * rows)
            hidden = jnp.concatenate(
                [
                    tok_ref[i * TILE_FRAMES + f].astype(F32)
                    + cond_ref[g0 + f].astype(F32) * embed_row
                    for f in range(TILE_FRAMES)
                ],
                axis=0,
            )
            mid = hidden + nn_dot(att_all[sl], wo_ref[...])
            mid_ref[sl] = jnp.concatenate(octets(mid, TILE_FRAMES, res), axis=0)
            mixer_in = rms_rows(mid, gain_row)
            mixer_in = jnp.concatenate(octets(mixer_in, TILE_FRAMES, res), axis=0).astype(BF16)
            mixed_ref[sl, width:] = nn_dot(mixer_in, wi_ref[:, width:]).astype(BF16)
            mixed_ref[sl, :width] = mixer_in
            tile_steps = steps_ref[i * TILE_FRAMES : (i + 1) * TILE_FRAMES]
            keep_end = [
                jnp.where((reset > g0 + f) & (reset <= g_end), 0.0, 1.0).astype(F32)
                for f in range(TILE_FRAMES)
            ]
            keep_all = jnp.where((reset >= g0) & (reset <= g_end), 0.0, 1.0).astype(F32)
            entry_ref[i] = s_ref[...].astype(BF16)
            reach_ref[i] = p_ref[...]
            for o in range(res // OCTET):
                os = slice(i * rows + o * half, i * rows + (o + 1) * half)
                st = tile_steps[:, o * OCTET : (o + 1) * OCTET].reshape(half, heads)
                decay = wide_decays(st, heads, width)
                after = [jnp.ones((OCTET, width), F32)]
                for f in range(TILE_FRAMES - 1, 0, -1):
                    after.append(after[-1] * frame_rows(decay, f))
                transit = after[-1] * frame_rows(decay, 0) * keep_all
                after = after[::-1]
                kept = jnp.concatenate([a * s for a, s in zip(after, keep_end)], axis=0)
                inner = mixed_ref[os, width : 2 * width].astype(F32)
                kept = (inner * kept).astype(BF16)
                maps = mixed_ref[os, 2 * width :].astype(F32)
                write_t = maps.T[:state]
                col = lax.broadcasted_iota(jnp.int32, (state, half), 1) % OCTET
                write = jnp.concatenate(
                    [jnp.where(col == r, write_t, 0.0).astype(BF16) for r in range(OCTET)], axis=0
                )
                added = nn_dot(write, kept)
                for r in range(OCTET):
                    rs = slice(r * state, (r + 1) * state)
                    ss = slice((o * OCTET + r) * state, (o * OCTET + r + 1) * state)
                    s_ref[ss] = s_ref[ss] * transit[r : r + 1] + added[rs]
                po = slice(o * OCTET, (o + 1) * OCTET)
                p_ref[po] = p_ref[po] * transit
        if not last:
            return
        p_all = p_ref[...]
        for r in range(res):
            p_wide[r] = jnp.broadcast_to(p_all[r : r + 1], (8, width))
        sub = lax.broadcasted_iota(jnp.int32, (CARRY_ROWS, width), 0) % 8
        for e in range(res // OCTET):
            for k in range(GROUP):
                r0 = e * OCTET + (place ^ k) * per_pay
                out = pay_refs[e * GROUP + k]
                start = pl.multiple_of(r0 * state, pay_rows)
                out[:pay_rows] = s_ref[pl.ds(start, pay_rows), :].astype(BF16)
                for n in range(0, per_pay, 2):
                    value = jnp.concatenate([p_wide[r0 + n], p_wide[r0 + n + 1]], axis=0)
                    upper = value.astype(BF16).astype(F32)
                    lo = pay_rows + n * 8
                    out[lo : lo + 16] = jnp.where(sub < 4, upper, value - upper).astype(BF16)

    chunk_rows = frames * res
    in_specs = (
        [SMEM_SPEC, whole(ids.shape)]
        + [pl.BlockSpec((frames, res, width), lambda i: (c, 0, 0))]
        + [whole(attended[0].shape)] * peers
        + [pl.BlockSpec((frames, res, heads), lambda i: (c, 0, 0))]
        + [whole(a.shape) for a in (embed, gain, w_out, w_in)]
        + [whole(a.shape) for a in carry_args]
        + [HBM_SPEC] * len(follow)
    )
    out_shape = [
        jax.ShapeDtypeStruct((chunk_rows, width), F32),
        jax.ShapeDtypeStruct((chunk_rows, mixed_width), BF16),
        jax.ShapeDtypeStruct((tiles, spread, width), BF16),
        jax.ShapeDtypeStruct((tiles, res, width), F32),
    ]
    scratch = [pltpu.VMEM((peers, part_frames, res, width), BF16)]
    if last:
        pay = (pay_rows + 8 * per_pay, width)
        out_shape += [jax.ShapeDtypeStruct(pay, BF16)] * pays
        scratch += [
            pltpu.VMEM((spread, width), F32),
            pltpu.VMEM((res, width), F32),
            pltpu.VMEM((res, 8, width), F32),
        ]
    else:
        out_shape += [
            jax.ShapeDtypeStruct((spread, width), F32),
            jax.ShapeDtypeStruct((res, width), F32),
        ]
    outs = pl.pallas_call(
        body,
        grid=(1,),
        in_specs=in_specs,
        out_specs=[whole(o.shape) for o in out_shape],
        out_shape=out_shape,
        scratch_shapes=scratch,
        compiler_params=grant(20),
        name="mix",
    )(cond, ids, tokens, *attended, steps, embed, gain, w_out, w_in, *carry_args, *follow)
    return outs[:4], outs[4:]


def scan_octet(o, c, frames_all, ids, skip, steps, mixed, entry, reach, w_in, mixer_scale):
    tiles, spread, width = entry.shape
    _, res, heads = steps.shape
    state = spread // res
    half = TILE_FRAMES * OCTET
    octet_state = OCTET * state
    octet_count = res // OCTET

    def body(
        ids_ref,
        skip_ref,
        steps_ref,
        mixed_ref,
        entry_ref,
        reach_ref,
        wg_ref,
        z_ref,
        ag_ref,
        rr_ref,
    ):
        reset = first_reset(ids_ref, frames_all)
        feature = lax.broadcasted_iota(jnp.int32, (1, width), 1) // (width // heads)
        skip_row = jnp.zeros((1, width), F32)
        for h in range(heads):
            skip_row = jnp.where(feature == h, skip_ref[h], skip_row)
        g0 = c * tiles * TILE_FRAMES + pl.program_id(0) * TILE_FRAMES
        row_i = lax.broadcasted_iota(jnp.int32, (half, half), 0)
        col_i = lax.broadcasted_iota(jnp.int32, (half, half), 1)
        edge = (reset - g0) * OCTET
        joined = (
            ((row_i % OCTET) == (col_i % OCTET))
            & (row_i >= col_i)
            & ((row_i >= edge) == (col_i >= edge))
        )
        keep_start = [
            jnp.where((reset >= g0) & (reset <= g0 + f), 0.0, 1.0).astype(F32)
            for f in range(TILE_FRAMES)
        ]
        decay = wide_decays(steps_ref[...].reshape(half, heads), heads, width)
        before = [frame_rows(decay, 0)]
        for f in range(1, TILE_FRAMES):
            before.append(before[-1] * frame_rows(decay, f))
        after = [jnp.ones((OCTET, width), F32)]
        for f in range(TILE_FRAMES - 1, 0, -1):
            after.append(after[-1] * frame_rows(decay, f))
        after = jnp.concatenate(after[::-1], axis=0)
        back = 1.0 / before[-1]
        relative = jnp.concatenate([b * back for b in before], axis=0)
        from_base = jnp.concatenate([b * s for b, s in zip(before, keep_start)], axis=0)
        inner = mixed_ref[:, width : 2 * width].astype(F32)
        ww, rr = twice_each(mixed_ref[:, 2 * width :].astype(F32), state)
        rr_ref[...] = rr.astype(BF16)
        gram = nt_dot(rr.astype(BF16), ww.astype(BF16)) * 0.5
        gram = jnp.where(joined, gram, 0.0).astype(BF16)
        near = nn_dot(gram, (inner * after).astype(BF16)) * relative
        far = nn_dot(spread_read(rr, state), entry_ref[0]) * from_base
        gate = nn_dot(mixed_ref[:, :width], wg_ref[...]).astype(BF16).astype(F32)
        gate = 0.5 * gate
        silu = gate + gate * jnp.tanh(gate)
        z_ref[...] = ((near + far) * mixer_scale + skip_row * inner) * silu
        start = reach_ref[0] * mixer_scale
        reached = jnp.concatenate(
            [start * frame_rows(from_base, f) for f in range(TILE_FRAMES)], axis=0
        )
        ag_ref[...] = (reached * silu).astype(BF16)

    total = tiles * half

    def row_block(cols):
        return pl.BlockSpec((half, cols), lambda i: (i, 0))

    return pl.pallas_call(
        body,
        grid=(tiles,),
        in_specs=[
            whole(ids.shape),
            SMEM_SPEC,
            pl.BlockSpec((TILE_FRAMES, OCTET, heads), lambda i: (c * tiles + i, o, 0)),
            pl.BlockSpec((half, mixed.shape[1]), lambda i: (i * octet_count + o, 0)),
            pl.BlockSpec((1, octet_state, width), lambda i: (i, o, 0)),
            pl.BlockSpec((1, OCTET, width), lambda i: (i, o, 0)),
            whole((width, width)),
        ],
        out_specs=[row_block(width), row_block(width), row_block(LANES)],
        out_shape=[
            jax.ShapeDtypeStruct((total, width), F32),
            jax.ShapeDtypeStruct((total, width), BF16),
            jax.ShapeDtypeStruct((total, LANES), BF16),
        ],
        compiler_params=grant(14),
        name="scan",
    )(ids, skip, steps, mixed, entry, reach, w_in)


def decay_rows(tail, n):
    tail = tail.astype(F32)
    return [tail[8 * i : 8 * i + 1] + tail[8 * i + 4 : 8 * i + 5] for i in range(n)]


def residues_of(pay, state):
    return pay // (state + 8)


def group_total(got, after, state):
    pay, width = got[0].shape
    n = residues_of(pay, state)
    body_rows = n * state

    def body(*refs):
        got_refs = refs[:GROUP]
        out_ref, sorted_s = refs[-2:]
        place = my_place()
        for k in range(GROUP):
            sorted_s[place ^ k] = got_refs[k][...]
        tails = [decay_rows(sorted_s[j, body_rows:], n) for j in range(GROUP)]
        sub = lax.broadcasted_iota(jnp.int32, (CARRY_ROWS, width), 0) % 8
        lines = []
        for i in range(n):
            rs = slice(i * state, (i + 1) * state)
            total = sorted_s[0, rs].astype(F32)
            product = tails[0][i]
            for j in range(1, GROUP):
                total = total * tails[j][i] + sorted_s[j, rs].astype(F32)
                product = product * tails[j][i]
            out_ref[rs] = total.astype(BF16)
            lines.append(jnp.broadcast_to(product, (8, width)))
        for i in range(0, n, 2):
            value = jnp.concatenate(lines[i : i + 2], axis=0)
            upper = value.astype(BF16).astype(F32)
            lo = body_rows + 8 * i
            out_ref[lo : lo + 16] = jnp.where(sub < 4, upper, value - upper).astype(BF16)

    return pl.pallas_call(
        body,
        grid=(1,),
        in_specs=[whole((pay, width))] * GROUP + [HBM_SPEC] * len(after),
        out_specs=whole((pay, width)),
        out_shape=jax.ShapeDtypeStruct((pay, width), BF16),
        scratch_shapes=[pltpu.VMEM((GROUP, pay, width), BF16)],
        compiler_params=grant(6),
        name="group_total",
    )(*got, *after)


def group_prefixes(got, entering, after, state):
    pay, width = got[0].shape
    n = residues_of(pay, state)
    body_rows = n * state

    def body(*refs):
        got_refs, in_ref = refs[:GROUP], refs[GROUP]
        out_refs = refs[-GROUP - 2 : -2]
        sorted_s, prefix_s = refs[-2:]
        place = my_place()
        for k in range(GROUP):
            sorted_s[place ^ k] = got_refs[k][...]
        tails = [decay_rows(sorted_s[j, body_rows:], n) for j in range(GROUP)]
        for i in range(n):
            rs = slice(i * state, (i + 1) * state)
            total = in_ref[rs].astype(F32)
            prefix_s[0, rs] = total.astype(BF16)
            for j in range(GROUP - 1):
                total = total * tails[j][i] + sorted_s[j, rs].astype(F32)
                prefix_s[j + 1, rs] = total.astype(BF16)
        for k in range(GROUP):
            out_refs[k][...] = prefix_s[place ^ k]

    spec = whole((pay, width))
    out = whole((body_rows, width))
    return pl.pallas_call(
        body,
        grid=(1,),
        in_specs=[spec] * (GROUP + 1) + [HBM_SPEC] * len(after),
        out_specs=[out] * GROUP,
        out_shape=[jax.ShapeDtypeStruct((body_rows, width), BF16)] * GROUP,
        scratch_shapes=[
            pltpu.VMEM((GROUP, pay, width), BF16),
            pltpu.VMEM((GROUP, body_rows, width), BF16),
        ],
        compiler_params=grant(8),
        name="group_prefixes",
    )(*got, entering, *after)


def join_payloads(earlier, later, state):
    n = residues_of(later.shape[0], state)
    body_rows = n * state
    width = later.shape[1]
    early = decay_rows(earlier[body_rows:], n)
    late = decay_rows(later[body_rows:], n)
    parts, lines = [], []
    for i in range(n):
        rs = slice(i * state, (i + 1) * state)
        parts.append(earlier[rs].astype(F32) * late[i] + later[rs].astype(F32))
        value = early[i] * late[i]
        upper = value.astype(BF16).astype(F32)
        lines += [jnp.broadcast_to(upper, (4, width)), jnp.broadcast_to(value - upper, (4, width))]
    return jnp.concatenate(parts + lines, axis=0).astype(BF16)


def states_entering(payloads, covers, state, tm_size):
    groups = tm_size // GROUP
    order = list(range(GROUP - 1, 0, -1))

    def swap(parts):
        moved = {
            k: lax.ppermute(parts[k], "tm", [(i, i ^ k) for i in range(tm_size)]) for k in order
        }
        return [parts[0]] + [moved[k] for k in range(1, GROUP)]

    def onward(value, hops):
        moved = hops * GROUP
        return lax.ppermute(value, "tm", [(i, i + moved) for i in range(tm_size - moved)])

    octet_count = len(payloads) // GROUP
    gathered = [swap(payloads[e * GROUP : (e + 1) * GROUP]) for e in range(octet_count)]
    result = []
    for e, got in enumerate(gathered):
        total = group_total(got, covers[e : e + 1], state)
        entering = onward(total, 1) if groups > 1 else jnp.zeros_like(total)
        hops = 1
        while hops < groups - 1:
            entering = join_payloads(onward(entering, hops), entering, state)
            hops *= 2
        result.append(swap(group_prefixes(got, entering, [], state)))
    return result


def finish_octet(o, entered, mids, scanned, w_mix, frames, res, state, ready):
    total, width = mids[0].shape
    octet_count = res // OCTET
    half = TILE_FRAMES * OCTET
    chunks = len(mids)
    tiles = total // (half * octet_count)
    rows = tiles * half
    piece = entered[0].shape[0]
    last = o == octet_count - 1

    def body(*refs):
        in_refs = refs[:GROUP]
        chunk_refs = refs[GROUP : GROUP + 4 * chunks]
        w_ref = refs[GROUP + 4 * chunks]
        ready_refs = refs[GROUP + 4 * chunks + 1 : -2]
        out_ref, state_s = refs[-2:]
        step = pl.program_id(0)

        @pl.when(step == 0)
        def _():
            place = my_place()
            for k in range(GROUP):
                state_s[place ^ k] = in_refs[k][...]

        def tile_of(c):
            mid_ref, z_ref, ag_ref, rr_ref = chunk_refs[4 * c : 4 * c + 4]
            read = spread_read(rr_ref[...].astype(F32), state)
            far = nn_dot(read, state_s[...].reshape(GROUP * piece, width))
            gated = (z_ref[...] + ag_ref[...].astype(F32) * far).astype(BF16)
            out = mid_ref[...].reshape(rows, width) + nn_dot(gated, w_ref[...])
            if not last:
                out_ref[...] = out.astype(BF16)
                return
            cubes = [r[...].astype(F32) for r in ready_refs] + [out]
            cubes = [x.reshape(tiles * TILE_FRAMES, OCTET, width) for x in cubes]
            out_ref[...] = jnp.concatenate(cubes, axis=1).astype(BF16)

        for c in range(chunks):
            pl.when(step == c)(lambda c=c: tile_of(c))

    chunk_args, chunk_specs = [], []
    for c in range(chunks):
        chunk_args += [mids[c].reshape(tiles, octet_count, half, width), *scanned[c]]
        chunk_specs.append(pl.BlockSpec((tiles, 1, half, width), lambda i: (0, o, 0, 0)))
        chunk_specs += [whole((rows, cols)) for cols in (width, width, LANES)]
    octet_rows = pl.BlockSpec((rows, width), lambda i: (i, 0))
    if last:
        out_spec = pl.BlockSpec((tiles * TILE_FRAMES, res, width), lambda i: (i, 0, 0))
        out_shape = jax.ShapeDtypeStruct((frames, res, width), BF16)
    else:
        out_spec = octet_rows
        out_shape = jax.ShapeDtypeStruct((chunks * rows, width), BF16)
    return pl.pallas_call(
        body,
        grid=(chunks,),
        in_specs=[whole((piece, width))] * GROUP
        + chunk_specs
        + [whole(w_mix.shape)]
        + [octet_rows] * len(ready),
        out_specs=out_spec,
        out_shape=out_shape,
        scratch_shapes=[pltpu.VMEM((GROUP, piece, width), BF16)],
        compiler_params=grant(20),
        name="finish",
    )(*entered, *chunk_args, w_mix, *ready)


def local(
    tokens,
    cond_mask,
    cond_embed,
    attn_gain,
    w_qkv,
    w_out,
    mix_gain,
    w_in,
    decay_steps,
    segment_ids,
    skip_gain,
    w_mix_out,
):
    frames, res, width = tokens.shape
    heads = skip_gain.shape[0]
    state = (w_in.shape[1] - 2 * width) // 2
    tm_size = lax.axis_size("tm")
    peers = lax.axis_size("res")
    part = PART_FRAMES
    chunks = frames // (part * peers)
    order = list(range(peers - 1, 0, -1))

    def swap(value, k):
        return lax.ppermute(value, "res", [(i, i ^ k) for i in range(peers)])

    ids = segment_ids.reshape(-1, LANES)
    pieces = prepare(tokens, [], chunks, peers)
    gathered = []
    for c in range(chunks):
        mine = pieces[c * peers : (c + 1) * peers]
        got = {k: swap(mine[k], k) for k in order}
        got[0] = mine[0]
        gathered.append([got[k] for k in range(peers)])

    embed = cond_embed.reshape(-1, LANES)
    first_gain = attn_gain.reshape(-1, LANES)
    second_gain = mix_gain.reshape(-1, LANES)
    mixer_scale = 1.0 / math.sqrt(frames * tm_size * state)

    attended = []
    for c in range(chunks):
        outs = attend_chunk(
            cond_mask,
            gathered[c],
            embed,
            first_gain,
            w_qkv,
            c * part * peers,
            heads,
            [] if c else [decay_steps],
        )
        back = {k: swap(outs[k], k) for k in order}
        back[0] = outs[0]
        attended.append([back[k] for k in range(peers)])

    octet_count = res // OCTET

    def scan(o, c):
        _, mixed, entry, reach = held[c]
        return scan_octet(
            o, c, frames, ids, skip_gain, decay_steps, mixed, entry, reach, w_in, mixer_scale
        )

    carry, held, scanned = None, [], []
    for c in range(chunks):
        after = [scanned[-1][0][2]] if scanned else []
        out, carry = mix_chunk(
            c,
            chunks,
            cond_mask,
            ids,
            tokens,
            attended[c],
            decay_steps,
            embed,
            second_gain,
            w_out,
            w_in,
            carry,
            after,
        )
        held.append(out)
        scanned.append([scan(o, c) for o in range(octet_count)])
    covers = [scanned[-1][0][2], scanned[0][-1][2]]
    entered = states_entering(carry, covers, state, tm_size)
    mids = [mid for mid, _, _, _ in held]
    ready = []
    for o in range(octet_count):
        parts = [scanned[c][o] for c in range(chunks)]
        done = finish_octet(o, entered[o], mids, parts, w_mix_out, frames, res, state, ready)
        ready = ready + [done]
    return done


def solution(mesh):
    in_specs = (
        P("tm", "res", None),
        P("tm"),
        P(),
        P(),
        P(),
        P(),
        P(),
        P(),
        P("tm", "res", None),
        P(),
        P(),
        P(),
    )
    out_specs = P("tm", "res", None)
    return jax.shard_map(local, mesh=mesh, in_specs=in_specs, out_specs=out_specs, check_vma=False)
```
